128 devices in a mesh: inp: 4 (over z), chan: 32 (over y, x, core).
Axes of the slice: x: 4, y: 4, z: 4, core: 2. Of those that a mesh axis runs over, the one named last changes fastest.
Arguments:
- samples: bfloat16 [1024, 512, 512], P('inp', 'chan'), may hold values from -16 to 16
- gram_owner: int32 [128], replicated, may hold values from 0 to 127, as said below
- beam_owner: int32 [256], replicated, may hold values from 0 to 31, as said below
- delays: float32 [256, 1024], replicated, may hold values from -64 to 64
- sections: int32 [256], replicated, may hold values from 0 to 255, each once
Outputs:
- visibilities: float32 [256, 2, 1024, 1024], P(('inp', 'chan'))
- beam_voltages: float32 [512, 4, 512, 128], P('chan', 'inp')
The draws below stay inside these ranges and needn't reach their ends.
Inputs may be any that keep to these rules, and one draw needn't show every extreme that they name: `gram_owner`: no device owns more than 2 of the correlated channels, and some device owns exactly 2. `beam_owner`: no index of chan owns more than 16 channels, and some owns exactly 16. `sections`: each value once.
All inputs are finite; a program needn't handle non-finite values.
Results may differ from the reference program's by a relative error of at most 0.0048.
Values may be sent and summed in bfloat16 or wider, within the bound.
No kernel may reach another device: no remote copies, remote signals or barrier semaphores. Data moves between devices by JAX's collectives and lax.ppermute only.
A program may use at most 256 MiB of HBM per device.

```python
import math
import jax
import jax.numpy as jnp
from jax import lax

WIDTH = 512
NCH = 256
XCH = 128
NIN = 1024
NBEAM = 256
FRAMES = 512
B_SEC = 64
XOWNERS = 128
XSLOTS = 2
BSLOTS = 16
N_INP = 4
N_CHAN = 32


def allot_owners(key, owner_count, slot_count, count):
    first_key, second_key, third_key = jax.random.split(key, 3)
    full_owner = jax.random.randint(first_key, (), 0, owner_count)
    order = jax.random.permutation(second_key, owner_count * slot_count)
    taken = (order // slot_count == full_owner).astype(jnp.int32)
    ranking = jnp.argsort(taken * (owner_count * slot_count) + jnp.arange(owner_count * slot_count), stable=True)
    remaining = order[ranking]
    picked = jnp.concatenate([full_owner * slot_count + jnp.arange(slot_count), remaining[:count - slot_count]])
    shuffle = jax.random.permutation(third_key, count)
    return (picked[shuffle] // slot_count).astype(jnp.int32)


def draw_gram_owner(key, part):
    return allot_owners(jax.random.fold_in(key, 11), XOWNERS, XSLOTS, XCH)


def draw_beam_owner(key, part):
    return allot_owners(jax.random.fold_in(key, 23), N_CHAN, BSLOTS, NCH)


def draw_samples(key, part):
    sky_key, gain_key, noise_key = jax.random.split(jax.random.fold_in(key, 37), 3)
    sky = jnp.clip(jax.random.normal(sky_key, (1, FRAMES, WIDTH), jnp.float32), -5.0, 5.0)
    gains = jax.random.uniform(gain_key, (NIN, 1, 1), jnp.float32, -1.5, 1.5)
    noise = jnp.clip(jax.random.normal(noise_key, (NIN, FRAMES, WIDTH), jnp.float32), -5.0, 5.0)
    return (gains * sky + noise).astype(jnp.bfloat16)


def setup_inputs(seed: int = 0) -> dict:
    seeds = jax.random.split(jax.random.key(seed), 6)
    return {
        "samples": draw_samples(jax.random.fold_in(seeds[5], 71), 0),
        "gram_owner": draw_gram_owner(jax.random.fold_in(seeds[5], 71), 0),
        "beam_owner": draw_beam_owner(jax.random.fold_in(seeds[5], 71), 0),
        "delays": jnp.clip(jax.random.uniform(seeds[3], (NBEAM, NIN), jnp.float32, -64.0, 64.0), -64.0, 64.0),
        "sections": jax.random.permutation(seeds[4], NBEAM).astype(jnp.int32),
    }


def fourier_table(length_total):
    half_count = length_total // 2
    rows = jnp.arange(half_count, dtype=jnp.int32)
    cols = jnp.arange(length_total, dtype=jnp.int32)
    turns = (rows[:, None] * cols[None, :] % length_total).astype(jnp.float32) * (2.0 * math.pi / length_total)
    factor = 1.0 / math.sqrt(length_total)
    return jnp.stack([jnp.cos(turns) * factor, -jnp.sin(turns) * factor]).astype(jnp.bfloat16)

def slot_table(owner_list, owner_count, slot_count):
    count = owner_list.shape[0]
    places = jnp.arange(count, dtype=jnp.int32)
    before = (owner_list[None, :] == owner_list[:, None]) & (places[None, :] < places[:, None])
    slot_of = lax.optimization_barrier(jnp.sum(before.astype(jnp.int32), axis=1)).astype(jnp.int32)
    keys = (owner_list * slot_count + slot_of).astype(jnp.int32)
    targets = jnp.arange(owner_count * slot_count, dtype=jnp.int32)
    match = keys[None, :] == targets[:, None]
    channel_of = lax.optimization_barrier(jnp.sum(jnp.where(match, places[None, :], 0), axis=1)).astype(jnp.int32)
    live_slot = jnp.any(match, axis=1)
    return (keys, channel_of, live_slot)

def reference(samples, gram_owner, beam_owner, delays, sections):
    table = fourier_table(WIDTH)
    spectra = jnp.einsum('pkw,ifw->kpfi', table.astype(jnp.float32), samples.astype(jnp.float32)).astype(jnp.bfloat16)
    gram_keys, _, _ = slot_table(gram_owner, XOWNERS, XSLOTS)

    def correlate(index):
        block = spectra[index]
        real_rows = block[0]
        imag_rows = block[1]
        real_part = jnp.dot(real_rows.T, real_rows, preferred_element_type=jnp.float32) + jnp.dot(imag_rows.T, imag_rows, preferred_element_type=jnp.float32)
        imag_part = jnp.dot(imag_rows.T, real_rows, preferred_element_type=jnp.float32) - jnp.dot(real_rows.T, imag_rows, preferred_element_type=jnp.float32)
        return jnp.stack([real_part, imag_part]) / FRAMES
    grams = lax.map(correlate, jnp.arange(XCH, dtype=jnp.int32))
    visibilities = jnp.zeros((XOWNERS * XSLOTS, 2, NIN, NIN), jnp.float32).at[gram_keys].set(grams)
    beam_keys, _, _ = slot_table(beam_owner, N_CHAN, BSLOTS)
    inverse = 1.0 / math.sqrt(NIN)

    def form(index):
        block = spectra[index]
        frequency = index.astype(jnp.float32)
        angle = frequency * delays * (2.0 * math.pi / WIDTH)
        real_weight = (jnp.cos(angle) * inverse).astype(jnp.bfloat16)
        imag_weight = (-jnp.sin(angle) * inverse).astype(jnp.bfloat16)
        real_beam = jnp.dot(block[0], real_weight.T, preferred_element_type=jnp.float32) - jnp.dot(block[1], imag_weight.T, preferred_element_type=jnp.float32)
        imag_beam = jnp.dot(block[1], real_weight.T, preferred_element_type=jnp.float32) + jnp.dot(block[0], imag_weight.T, preferred_element_type=jnp.float32)
        both = jnp.stack([real_beam, imag_beam], axis=1)
        both = jnp.take(both, sections, axis=2).reshape(FRAMES, 2, N_INP, B_SEC)
        return jnp.transpose(both, (2, 0, 1, 3)).reshape(N_INP, FRAMES, 2 * B_SEC)
    formed = lax.map(form, jnp.arange(NCH, dtype=jnp.int32))
    beam_voltages = jnp.zeros((N_CHAN * BSLOTS, N_INP, FRAMES, 2 * B_SEC), jnp.float32).at[beam_keys].set(formed)
    return (visibilities, beam_voltages)
```

```python
import functools
import math

import jax
import jax.numpy as jnp
import ml_dtypes
import numpy as np
from jax import lax
from jax.experimental import pallas as pl
from jax.experimental.pallas import tpu as pltpu
from jax.sharding import PartitionSpec as P

BF16 = jnp.bfloat16
F32 = jnp.float32
VMEM_LIMIT = 56 * 1024 * 1024


def fourier_table(length_total):
    half_count = length_total // 2
    rows = np.arange(half_count, dtype=np.int32)
    cols = np.arange(length_total, dtype=np.int32)
    turns = (rows[:, None] * cols[None, :] % length_total).astype(np.float32)
    turns = turns * np.float32(2.0 * math.pi / length_total)
    factor = np.float32(1.0 / math.sqrt(length_total))
    both = np.stack([np.cos(turns) * factor, -np.sin(turns) * factor], axis=1)
    return both.reshape(length_total, length_total).astype(ml_dtypes.bfloat16)


def frame_major(frames):
    count = frames * frames
    matrix = np.zeros((count, count), np.float32)
    for f in range(frames):
        for i in range(frames):
            matrix[f * frames + i, i * frames + f] = 1.0
    return matrix.astype(ml_dtypes.bfloat16)


def params(**more):
    return pltpu.CompilerParams(vmem_limit_bytes=VMEM_LIMIT, **more)


def vmem():
    return pl.BlockSpec(memory_space=pltpu.VMEM)


def smem():
    return pl.BlockSpec(memory_space=pltpu.SMEM)


def channelize_body(
    slots, owner_ref, x_ref, table_ref, perm_ref, gram_ref, spec_ref, xs, rows, taken
):
    frames, inputs, width = xs.shape
    channels = spec_ref.shape[0]
    gram_channels = owner_ref.shape[0]

    def clear(o, carry):
        taken[o] = 0
        return carry

    lax.fori_loop(0, taken.shape[0], clear, 0)

    group = frames * frames

    def reorder(b, carry):
        block = x_ref[pl.ds(pl.multiple_of(b * group, group), group), :]
        moved = jnp.dot(perm_ref[...], block, preferred_element_type=F32)
        moved = moved.astype(BF16).reshape(frames, frames, width)
        xs[:, pl.ds(pl.multiple_of(b * frames, frames), frames), :] = moved
        return carry

    lax.fori_loop(0, inputs // frames, reorder, 0, unroll=2)

    def transform(f, carry):
        out = lax.dot_general(
            table_ref[...], xs[f], (((1,), (1,)), ((), ())), preferred_element_type=F32
        )
        for half in range(inputs // 128):
            rows[half, pl.ds(f, 2 * channels, stride=frames), :] = out[
                :, half * 128 : half * 128 + 128
            ]
        return carry

    lax.fori_loop(0, frames, transform, 0)

    def fetch(k):
        start = pl.multiple_of(k * 2 * frames, 2 * frames)
        both = [rows[h, pl.ds(start, 2 * frames), :] for h in range(inputs // 128)]
        return jnp.concatenate(both, axis=1).astype(BF16).reshape(2, frames, inputs)

    def low(k, carry):
        owner = owner_ref[k]
        slot = taken[owner]
        taken[owner] = slot + 1
        value = fetch(k)
        spec_ref[k] = value
        gram_ref[owner * slots + slot] = value
        return carry

    lax.fori_loop(0, gram_channels, low, 0, unroll=4)

    def high(k, carry):
        spec_ref[k] = fetch(k)
        return carry

    lax.fori_loop(gram_channels, channels, high, 0, unroll=4)


def channelize(samples, gram_owner, owner_count, slots):
    inputs, frames, width = samples.shape
    channels = width // 2
    return pl.pallas_call(
        functools.partial(channelize_body, slots),
        out_shape=(
            jax.ShapeDtypeStruct((owner_count * slots, 2, frames, inputs), BF16),
            jax.ShapeDtypeStruct((channels, 2, frames, inputs), BF16),
        ),
        in_specs=[smem(), vmem(), vmem(), vmem()],
        out_specs=(vmem(), vmem()),
        scratch_shapes=[
            pltpu.VMEM((frames, inputs, width), BF16),
            pltpu.VMEM((inputs // 128, 2 * channels * frames, 128), F32),
            pltpu.SMEM((owner_count,), jnp.int32),
        ],
        compiler_params=params(),
        name="channelize",
    )(
        gram_owner,
        samples.reshape(inputs * frames, width),
        jnp.asarray(fourier_table(width)),
        jnp.asarray(frame_major(frames)),
    )


STEP = 16


def turn(a, b, c, s):
    return a * c - b * s, b * c + a * s


def beam_body(
    first, lanes_half, spec_ref, cos_ref, sin_ref, keep_ref, a_ref, a2_ref, b_ref, b2_ref,
    cm, sm, big_c, big_s, now_c, now_s, weights,
):
    step = pl.program_id(0)
    steps = pl.num_programs(0)
    inputs, lanes = cos_ref.shape
    frames = keep_ref.shape[1]
    tiles = lanes // 128
    half = STEP // 2

    @pl.when(step == 0)
    def _():
        def start(r, carry):
            rows = pl.ds(pl.multiple_of(r * 8, 8), 8)
            for t in range(tiles):
                cols = pl.ds(t * 128, 128)
                c1, s1 = cos_ref[rows, cols], sin_ref[rows, cols]
                c, s = c1, s1
                powers = [(c1, s1)]
                cm[0, rows, cols] = c
                sm[0, rows, cols] = s
                for m in range(2, half + 1):
                    x, y = powers[m // 2 - 1], powers[m - m // 2 - 1]
                    c, s = turn(x[0], x[1], y[0], y[1])
                    powers.append((c, s))
                    cm[m - 1, rows, cols] = c
                    sm[m - 1, rows, cols] = s
                c8, s8 = powers[half - 1]
                c16, s16 = turn(c8, s8, c8, s8)
                big_c[rows, cols] = c16
                big_s[rows, cols] = s16
                a, b = c8, s8
                if first:
                    c, s = c16, s16
                    done = STEP
                    while done < first:
                        c, s = turn(c, s, c, s)
                        done *= 2
                    a, b = turn(a, b, c, s)
                lane = lax.broadcasted_iota(jnp.int32, a.shape, 1)
                real = lane < lanes_half
                scale = 1.0 / 32.0
                now_c[rows, cols] = jnp.where(real, a, -b) * scale
                now_s[rows, cols] = jnp.where(real, b, a) * scale
            return carry

        lax.fori_loop(0, inputs // 8, start, 0)

    def make(r, carry):
        rows = pl.ds(pl.multiple_of(r * 16, 16), 16)
        for t in range(tiles):
            cols = pl.ds(t * 128, 128)
            a, b = now_c[rows, cols], now_s[rows, cols]
            weights[half, rows, cols] = a.astype(BF16)
            for m in range(1, half + 1):
                p = a * cm[m - 1, rows, cols]
                q = b * sm[m - 1, rows, cols]
                weights[half - m, rows, cols] = (p + q).astype(BF16)
                if m < half:
                    weights[half + m, rows, cols] = (p - q).astype(BF16)
            c16, s16 = big_c[rows, cols], big_s[rows, cols]
            now_c[rows, cols], now_s[rows, cols] = turn(a, b, c16, s16)
        return carry

    lax.fori_loop(0, inputs // 16, make, 0)

    lane = lax.broadcasted_iota(jnp.int32, (frames, 128), 1)
    sign = jnp.where(lane < lanes_half, -1.0, 1.0).astype(F32)
    outs = []
    for m in range(STEP):
        got = jnp.dot(spec_ref[m], weights[m], preferred_element_type=F32)
        parts = []
        for t in range(tiles):
            real = got[:frames, t * 128 : t * 128 + 128]
            imag = got[frames:, t * 128 : t * 128 + 128]
            parts.append((real + sign * pltpu.roll(imag, 64, 1)).astype(BF16))
        outs.append(parts)
    for m in range(STEP):
        keep_ref[step * STEP + m] = outs[m][0]

    @pl.when(step < steps // 2)
    def _():
        for m in range(STEP):
            at = step * STEP + m
            a_ref[0, at] = outs[m][1]
            a_ref[1, at] = outs[m][3]
            a2_ref[at] = outs[m][2]

    @pl.when(step >= steps // 2)
    def _():
        for m in range(STEP):
            at = (step - steps // 2) * STEP + m
            b_ref[0, at] = outs[m][2]
            b_ref[1, at] = outs[m][3]
            b2_ref[at] = outs[m][1]


def beamform(spectra, cosines, sines, first, count):
    channels, _, frames, inputs = spectra.shape
    lanes = cosines.shape[1]
    part = count // 2
    tile = (frames, 128)
    spectra = spectra.reshape(channels, 2 * frames, inputs)
    table = pltpu.VMEM((STEP // 2, inputs, lanes), F32)
    state = pltpu.VMEM((inputs, lanes), F32)
    whole = lambda *shape: pl.BlockSpec(shape, lambda j: (0,) * len(shape))
    flops = count * 2 * (2 * frames) * inputs * lanes
    return pl.pallas_call(
        functools.partial(beam_body, first, 64),
        grid=(count // STEP,),
        out_shape=(
            jax.ShapeDtypeStruct((count, *tile), BF16),
            jax.ShapeDtypeStruct((2, part, *tile), BF16),
            jax.ShapeDtypeStruct((part, *tile), BF16),
            jax.ShapeDtypeStruct((2, part, *tile), BF16),
            jax.ShapeDtypeStruct((part, *tile), BF16),
        ),
        in_specs=[
            pl.BlockSpec((STEP, 2 * frames, inputs), lambda j: (first // STEP + j, 0, 0)),
            whole(inputs, lanes),
            whole(inputs, lanes),
        ],
        out_specs=(
            whole(count, *tile),
            whole(2, part, *tile),
            whole(part, *tile),
            whole(2, part, *tile),
            whole(part, *tile),
        ),
        scratch_shapes=[
            table, table, state, state, state, state,
            pltpu.VMEM((STEP, inputs, lanes), BF16),
        ],
        compiler_params=params(dimension_semantics=("arbitrary",)),
        cost_estimate=pl.CostEstimate(
            flops=8 * flops, bytes_accessed=count * 2 * frames * inputs * 4, transcendentals=0
        ),
        name=f"beamform_{first}",
    )(spectra, cosines, sines)


def place_body(slots, chunks, owner_ref, *refs):
    ins, out_ref, taken = refs[:-2], refs[-2], refs[-1]

    def clear(o, carry):
        taken[o] = 0
        return carry

    lax.fori_loop(0, taken.shape[0], clear, 0)
    base = 0
    for c in range(chunks):
        keep, *rest = ins[c * 5 : c * 5 + 5]
        part = rest[0].shape[1]
        for h in range(2):
            near, far = rest[2 * h], rest[2 * h + 1]

            def body(n, carry, h=h, near=near, far=far, keep=keep, base=base, part=part):
                k = base + h * part + n
                owner = owner_ref[k]
                slot = taken[owner]
                taken[owner] = slot + 1
                total = keep[h * part + n].astype(F32) + near[0, n].astype(F32)
                total = total + far[n].astype(F32)
                out_ref[owner * slots + slot] = total.astype(BF16)
                return carry

            lax.fori_loop(0, part, body, 0, unroll=4)
        base += 2 * part


def place(beam_owner, groups, owner_count, slots):
    flat = [a for g in groups for a in g]
    tile = groups[0][0].shape[1:]
    return pl.pallas_call(
        functools.partial(place_body, slots, len(groups)),
        out_shape=jax.ShapeDtypeStruct((owner_count * slots, *tile), BF16),
        in_specs=[smem()] + [vmem()] * len(flat),
        out_specs=vmem(),
        scratch_shapes=[pltpu.SMEM((owner_count,), jnp.int32)],
        compiler_params=params(),
        name="place_beams",
    )(beam_owner, *flat)


def deliver_body(live_ref, x_ref, o_ref):
    slot = pl.program_id(0)
    sources, _, frames, lanes = x_ref.shape

    @pl.when(slot < live_ref[0])
    def _():
        o_ref[0] = x_ref[:, 0].astype(F32).reshape(sources * frames, lanes)

    @pl.when(slot >= live_ref[0])
    def _():
        o_ref[0] = jnp.zeros((sources * frames, lanes), F32)


def deliver(live, arrived, sources, slots):
    _, frames, lanes = arrived.shape
    return pl.pallas_call(
        deliver_body,
        grid=(slots,),
        out_shape=jax.ShapeDtypeStruct((slots, sources * frames, lanes), F32),
        in_specs=[
            smem(),
            pl.BlockSpec((sources, 1, frames, lanes), lambda s: (0, s, 0, 0)),
        ],
        out_specs=pl.BlockSpec((1, sources * frames, lanes), lambda s: (s, 0, 0)),
        compiler_params=params(dimension_semantics=("arbitrary",)),
        name="deliver_beams",
    )(live, arrived.reshape(sources, slots, frames, lanes))


def gram_body(scale, groups, live_ref, x_ref, o_ref):
    slot, row = pl.program_id(0), pl.program_id(1)
    sources, _, _, frames, inputs = x_ref.shape
    each = sources // groups
    depth = each * frames
    over = (((0,), (0,)), ((), ()))

    @pl.when(slot < live_ref[0])
    def _():
        mine = pl.ds(row * each, each)
        r_a = x_ref[mine, 0, 0].reshape(depth, inputs)
        m_a = x_ref[mine, 0, 1].reshape(depth, inputs)
        left_re = jnp.concatenate([r_a, m_a], axis=0)
        left_im = jnp.concatenate([m_a, -r_a], axis=0)
        for b in range(groups):
            r_b = x_ref[b * each : b * each + each, 0, 0].reshape(depth, inputs)
            m_b = x_ref[b * each : b * each + each, 0, 1].reshape(depth, inputs)
            right = jnp.concatenate([r_b, m_b], axis=0)
            cols = pl.ds(b * inputs, inputs)
            re = lax.dot_general(left_re, right, over, preferred_element_type=F32)
            im = lax.dot_general(left_im, right, over, preferred_element_type=F32)
            o_ref[0, 0, :, cols] = re * scale
            o_ref[0, 1, :, cols] = im * scale

    @pl.when(slot >= live_ref[0])
    def _():
        o_ref[...] = jnp.zeros_like(o_ref)


def gram(live, arrived, groups, sources, slots):
    _, _, frames, inputs = arrived.shape
    total = groups * inputs
    scale = 1.0 / (sources // groups * frames)
    return pl.pallas_call(
        functools.partial(gram_body, scale, groups),
        grid=(slots, groups),
        out_shape=jax.ShapeDtypeStruct((slots, 2, total, total), F32),
        in_specs=[
            smem(),
            pl.BlockSpec((sources, 1, 2, frames, inputs), lambda s, a: (0, s, 0, 0, 0)),
        ],
        out_specs=pl.BlockSpec((1, 2, inputs, total), lambda s, a: (s, 0, a, 0)),
        compiler_params=params(dimension_semantics=("arbitrary", "arbitrary")),
        cost_estimate=pl.CostEstimate(
            flops=slots * 8 * total * total * (sources // groups) * frames,
            bytes_accessed=slots * 12 * total * total,
            transcendentals=0,
        ),
        name="gram",
    )(live, arrived.reshape(sources, slots, 2, frames, inputs))


def shards(samples, gram_owner, beam_owner, delays, sections):
    input_count, frame_count, length_total = samples.shape
    half_count = length_total // 2
    inp_count = lax.axis_size("inp")
    chan_count = lax.axis_size("chan")
    inp_here = lax.axis_index("inp")
    chan_here = lax.axis_index("chan")
    owner_count = inp_count * chan_count
    gram_slots = 2 * gram_owner.shape[0] // owner_count
    beam_slots = 2 * half_count // chan_count
    beam_total = delays.shape[0]
    section_width = beam_total // inp_count

    outgoing, spectra = channelize(samples, gram_owner, owner_count, gram_slots)
    arrived = lax.all_to_all(outgoing, ("inp", "chan"), split_axis=0, concat_axis=0, tiled=True)

    order = jnp.stack([inp_here, inp_here ^ 1, 3 - inp_here, 3 - (inp_here ^ 1)])
    beams = sections.reshape(inp_count, section_width)[order].reshape(-1)
    delay_cols = lax.dynamic_slice_in_dim(delays, inp_here * input_count, input_count, 1)
    theta = jnp.take(delay_cols, beams, axis=0) * (2.0 * math.pi / length_total)
    theta = theta.T.reshape(input_count, inp_count, 1, section_width)

    def lanes_of(values):
        shape = (input_count, inp_count, 2, section_width)
        return jnp.broadcast_to(values, shape).reshape(input_count, 2 * beam_total)

    cosines, sines = lanes_of(jnp.cos(theta)), lanes_of(jnp.sin(theta))

    side = [(z, z ^ 1) for z in range(inp_count)]
    back = [(z, 3 - z) for z in range(inp_count)]
    chunk = half_count // 2
    groups = []
    for first in range(0, half_count, chunk):
        keep, a, a2, b, b2 = beamform(spectra, cosines, sines, first, chunk)
        a_in = lax.ppermute(a, "inp", side)
        b_in = lax.ppermute(b, "inp", back)
        a_sum = (a2.astype(F32) + a_in[1].astype(F32)).astype(BF16)
        b_sum = (b2.astype(F32) + b_in[1].astype(F32)).astype(BF16)
        a_far = lax.ppermute(a_sum, "inp", back)
        b_far = lax.ppermute(b_sum, "inp", side)
        groups.append((keep, a_in, a_far, b_in, b_far))
    leaving = place(beam_owner, groups, chan_count, beam_slots)
    leaving, arrived = lax.optimization_barrier((leaving, arrived))
    beams_in = lax.all_to_all(leaving, "chan", split_axis=0, concat_axis=0, tiled=True)

    here = inp_here * chan_count + chan_here
    gram_live = jnp.sum((gram_owner == here).astype(jnp.int32)).reshape(1)
    beam_live = jnp.sum((beam_owner == chan_here).astype(jnp.int32)).reshape(1)
    visibilities = gram(gram_live, arrived, inp_count, owner_count, gram_slots)
    formed = deliver(beam_live, beams_in, chan_count, beam_slots)
    return (visibilities, formed[:, None])


def solution(mesh):
    return jax.shard_map(
        shards,
        mesh=mesh,
        in_specs=(P("inp", "chan", None), P(), P(), P(), P()),
        out_specs=(P(("inp", "chan"), None, None, None), P("chan", "inp", None, None)),
        check_vma=False,
    )
```

```python
import functools
import math

import jax
import jax.numpy as jnp
import ml_dtypes
import numpy as np
from jax import lax
from jax.experimental import pallas as pl
from jax.experimental.pallas import tpu as pltpu
from jax.sharding import PartitionSpec as P

BF16 = jnp.bfloat16
F32 = jnp.float32
VMEM_LIMIT = 56 * 1024 * 1024


def fourier_table(length_total):
    half_count = length_total // 2
    rows = np.arange(half_count, dtype=np.int32)
    cols = np.arange(length_total, dtype=np.int32)
    turns = (rows[:, None] * cols[None, :] % length_total).astype(np.float32)
    turns = turns * np.float32(2.0 * math.pi / length_total)
    factor = np.float32(1.0 / math.sqrt(length_total))
    both = np.stack([np.cos(turns) * factor, -np.sin(turns) * factor], axis=1)
    return both.reshape(length_total, length_total).astype(ml_dtypes.bfloat16)


def frame_major(frames):
    count = frames * frames
    matrix = np.zeros((count, count), np.float32)
    for f in range(frames):
        for i in range(frames):
            matrix[f * frames + i, i * frames + f] = 1.0
    return matrix.astype(ml_dtypes.bfloat16)


def params(**more):
    return pltpu.CompilerParams(vmem_limit_bytes=VMEM_LIMIT, **more)


def vmem():
    return pl.BlockSpec(memory_space=pltpu.VMEM)


def smem():
    return pl.BlockSpec(memory_space=pltpu.SMEM)


CHUNKS = 4
PIECE = 32


def channelize_body(
    slots, owner_ref, x_hbm, table_ref, perm_ref, gram_hbm, spec_hbm,
    x_ref, xs, rows, spec, taken, in_sem, gram_sem, spec_sem,
):
    frames, inputs, width = xs.shape
    channels = spec.shape[0]
    gram_channels = owner_ref.shape[0]
    group = frames * frames
    piece = inputs * frames // CHUNKS
    loads = []
    for c in range(CHUNKS):
        part = pl.ds(c * piece, piece)
        loads.append(pltpu.make_async_copy(x_hbm.at[part], x_ref.at[part], in_sem.at[c]))
        loads[-1].start()

    def clear(o, carry):
        taken[o] = 0
        return carry

    lax.fori_loop(0, taken.shape[0], clear, 0)

    def reorder(b, carry):
        block = x_ref[pl.ds(pl.multiple_of(b * group, group), group), :]
        moved = jnp.dot(perm_ref[...], block, preferred_element_type=F32)
        moved = moved.astype(BF16).reshape(frames, frames, width)
        xs[:, pl.ds(pl.multiple_of(b * frames, frames), frames), :] = moved
        return carry

    blocks = piece // group
    for c in range(CHUNKS):
        loads[c].wait()
        lax.fori_loop(c * blocks, (c + 1) * blocks, reorder, 0, unroll=True)

    def fetch(k):
        start = pl.multiple_of(k * 2 * frames, 2 * frames)
        both = [rows[h, pl.ds(start, 2 * frames), :] for h in range(inputs // 128)]
        return jnp.concatenate(both, axis=1).astype(BF16).reshape(2, frames, inputs)

    def low(k, carry):
        owner = owner_ref[k]
        slot = taken[owner]
        taken[owner] = slot + 1
        spec[k] = fetch(k)
        pltpu.make_async_copy(spec.at[k], gram_hbm.at[owner * slots + slot], gram_sem).start()
        return carry

    def high(k, carry):
        spec[k] = fetch(k)
        return carry

    saves = []
    for start in range(0, channels, gram_channels):
        count = min(gram_channels, channels - start)

        def transform(f, carry, start=start, count=count):
            out = lax.dot_general(
                table_ref[2 * start : 2 * (start + count)],
                xs[f],
                (((1,), (1,)), ((), ())),
                preferred_element_type=F32,
            )
            for h in range(inputs // 128):
                at = pl.ds(f + 2 * start * frames, 2 * count, stride=frames)
                rows[h, at, :] = out[:, h * 128 : h * 128 + 128]
            return carry

        lax.fori_loop(0, frames, transform, 0, unroll=4)
        for k in range(start, start + count, PIECE):
            lax.fori_loop(k, k + PIECE, high if start else low, 0, unroll=4)
            part = pl.ds(k, PIECE)
            saves.append(pltpu.make_async_copy(spec.at[part], spec_hbm.at[part], spec_sem.at[k // PIECE]))
            saves[-1].start()
    all_low = pl.ds(0, gram_channels)
    pltpu.make_async_copy(spec.at[all_low], gram_hbm.at[all_low], gram_sem).wait()
    for save in saves:
        save.wait()


def channelize(samples, gram_owner, owner_count, slots):
    inputs, frames, width = samples.shape
    channels = width // 2
    anywhere = pl.BlockSpec(memory_space=pl.ANY)
    return pl.pallas_call(
        functools.partial(channelize_body, slots),
        out_shape=(
            jax.ShapeDtypeStruct((owner_count * slots, 2, frames, inputs), BF16),
            jax.ShapeDtypeStruct((channels, 2, frames, inputs), BF16),
        ),
        in_specs=[smem(), anywhere, vmem(), vmem()],
        out_specs=(anywhere, anywhere),
        scratch_shapes=[
            pltpu.VMEM((inputs * frames, width), BF16),
            pltpu.VMEM((frames, inputs, width), BF16),
            pltpu.VMEM((inputs // 128, 2 * channels * frames, 128), F32),
            pltpu.VMEM((channels, 2, frames, inputs), BF16),
            pltpu.SMEM((owner_count,), jnp.int32),
            pltpu.SemaphoreType.DMA((CHUNKS,)),
            pltpu.SemaphoreType.DMA(()),
            pltpu.SemaphoreType.DMA((channels // PIECE,)),
        ],
        compiler_params=params(),
        name="channelize",
    )(
        gram_owner,
        samples.reshape(inputs * frames, width),
        jnp.asarray(fourier_table(width)),
        jnp.asarray(frame_major(frames)),
    )


def small_turn(angle):
    square = angle * angle
    cosine = sine = jnp.zeros_like(angle)
    for n in range(6, 0, -1):
        cosine = (cosine + (-1.0) ** n / math.factorial(2 * n)) * square
        sine = (sine + (-1.0) ** n / math.factorial(2 * n + 1)) * square
    return 1.0 + cosine, angle + angle * sine


def phase_body(factor, half, inp_ref, section_ref, delay_ref, cos_ref, sin_ref, turned):
    here = inp_ref[0]
    near = jnp.bitwise_xor(here, 1)
    for q, device in enumerate((here, near, 3 - here, 3 - near)):

        def row(t, carry, q=q, device=device):
            beam = section_ref[device * half + t]
            turned[pl.ds(q * half + t, 1), :] = delay_ref[pl.ds(beam, 1), :]
            return carry

        lax.fori_loop(0, half, row, 0, unroll=8)
    for q in range(turned.shape[0] // half):
        cosines, sines = small_turn(turned[q * half : q * half + half] * factor)
        for source, target in ((cosines, cos_ref), (sines, sin_ref)):
            rows = jnp.concatenate([source, source], axis=0).T
            target[:, q * 2 * half : (q + 1) * 2 * half] = rows


def phases(inp_here, sections, delays, inputs, half, factor):
    beams = delays.shape[0]
    return pl.pallas_call(
        functools.partial(phase_body, factor, half),
        grid_spec=pltpu.PrefetchScalarGridSpec(
            num_scalar_prefetch=2,
            grid=(1,),
            in_specs=[pl.BlockSpec((beams, inputs), lambda g, inp, sec: (0, inp[0]))],
            out_specs=[pl.BlockSpec((inputs, 2 * beams), lambda g, inp, sec: (0, 0))] * 2,
            scratch_shapes=[pltpu.VMEM((beams, inputs), F32)],
        ),
        out_shape=[jax.ShapeDtypeStruct((inputs, 2 * beams), F32)] * 2,
        compiler_params=params(),
        name="phases",
    )(inp_here.reshape(1), sections, delays)


STEP = 16


def turn(a, b, c, s):
    return a * c - b * s, b * c + a * s


def beam_body(
    first, half, spec_ref, cos_ref, sin_ref, keep_ref, a_ref, a2_ref, b_ref, b2_ref,
    big_c, big_s, now_c, now_s, even, odd, stage,
):
    step = pl.program_id(0)
    last = pl.num_programs(0) - 1
    inputs, lanes = cos_ref.shape
    frames = keep_ref.shape[1]
    tiles = lanes // 128

    @pl.when(step == 0)
    def _():
        def start(r, carry):
            rows = pl.ds(pl.multiple_of(r * 16, 16), 16)
            for t in range(tiles):
                cols = pl.ds(t * 128, 128)
                c, s = cos_ref[rows, cols], sin_ref[rows, cols]
                done = 1
                while done < STEP // 2:
                    c, s = turn(c, s, c, s)
                    done *= 2
                mid = c, s
                c, s = turn(c, s, c, s)
                done *= 2
                big_c[rows, cols] = c
                big_s[rows, cols] = s
                while done < first:
                    c, s = turn(c, s, c, s)
                    done *= 2
                c, s = turn(*mid, c, s) if first else mid
                lane = lax.broadcasted_iota(jnp.int32, c.shape, 1)
                scale = 1.0 / 32.0
                now_c[rows, cols] = jnp.where(lane < half, c, -s) * scale
                now_s[rows, cols] = jnp.where(lane < half, s, c) * scale
            return carry

        lax.fori_loop(0, inputs // 16, start, 0)

    def make(r, weights):
        rows = pl.ds(pl.multiple_of(r * 16, 16), 16)
        a, b = now_c[rows], now_s[rows]
        c1, s1 = cos_ref[rows], sin_ref[rows]
        twice = c1 + c1
        p, q = a * c1, b * s1
        below, above = (a, p + q), (a, p - q)
        mid = STEP // 2
        weights[mid, rows] = a.astype(BF16)
        for m in range(1, mid + 1):
            weights[mid - m, rows] = below[1].astype(BF16)
            if m < mid:
                weights[mid + m, rows] = above[1].astype(BF16)
                below = below[1], twice * below[1] - below[0]
                above = above[1], twice * above[1] - above[0]
        now_c[rows], now_s[rows] = turn(a, b, big_c[rows], big_s[rows])

    lane = lax.broadcasted_iota(jnp.int32, (frames, 128), 1)
    sign = jnp.where(lane < half, -1.0, 1.0).astype(F32)

    def form(m, weights):
        got = jnp.dot(spec_ref[m], weights[m], preferred_element_type=F32)
        parts = []
        for t in range(tiles):
            real = got[:frames, t * 128 : t * 128 + 128]
            imag = got[frames:, t * 128 : t * 128 + 128]
            parts.append((real + sign * pltpu.roll(imag, half, 1)).astype(BF16))
        keep_ref[m] = parts[0]
        for t in range(1, tiles):
            stage[t - 1, m] = parts[t]

    @pl.when(step == 0)
    def _():
        @pl.loop(0, inputs // 16, unroll=2)
        def _(r):
            make(r, even)

    @pl.when((step > 0) & (step < last) & (step % 2 == 1))
    def _():
        @pl.loop(0, STEP, unroll=True)
        def _(r):
            form(r, even)
            make(r, odd)

    @pl.when((step > 0) & (step < last) & (step % 2 == 0))
    def _():
        @pl.loop(0, STEP, unroll=True)
        def _(r):
            form(r, odd)
            make(r, even)

    @pl.when(step == last)
    def _():
        @pl.loop(0, STEP, unroll=True)
        def _(r):
            form(r, odd)

    middle = last // 2

    @pl.when((step > 0) & (step <= middle))
    def _():
        a_ref[0], a_ref[1], a2_ref[...] = stage[0], stage[2], stage[1]

    @pl.when(step > middle)
    def _():
        b_ref[0], b_ref[1], b2_ref[...] = stage[1], stage[2], stage[0]


def beamform(spectra, cosines, sines, first, count):
    channels, _, frames, inputs = spectra.shape
    lanes = cosines.shape[1]
    part = count // 2
    tile = (frames, 128)
    steps = count // STEP
    assert steps % 2 == 0 and inputs // 16 == STEP
    spectra = spectra.reshape(channels, 2 * frames, inputs)
    state = pltpu.VMEM((inputs, lanes), F32)
    at = lambda j: jnp.maximum(j - 1, 0)
    low = lambda j: jnp.minimum(at(j), steps // 2 - 1)
    high = lambda j: jnp.maximum(at(j) - steps // 2, 0)
    whole = lambda *shape: pl.BlockSpec(shape, lambda j: (0,) * len(shape))
    flops = count * 2 * (2 * frames) * inputs * lanes
    return pl.pallas_call(
        functools.partial(beam_body, first, 64),
        grid=(steps + 1,),
        out_shape=(
            jax.ShapeDtypeStruct((count, *tile), BF16),
            jax.ShapeDtypeStruct((2, part, *tile), BF16),
            jax.ShapeDtypeStruct((part, *tile), BF16),
            jax.ShapeDtypeStruct((2, part, *tile), BF16),
            jax.ShapeDtypeStruct((part, *tile), BF16),
        ),
        in_specs=[
            pl.BlockSpec((STEP, 2 * frames, inputs), lambda j: (first // STEP + at(j), 0, 0)),
            whole(inputs, lanes),
            whole(inputs, lanes),
        ],
        out_specs=(
            pl.BlockSpec((STEP, *tile), lambda j: (at(j), 0, 0)),
            pl.BlockSpec((2, STEP, *tile), lambda j: (0, low(j), 0, 0)),
            pl.BlockSpec((STEP, *tile), lambda j: (low(j), 0, 0)),
            pl.BlockSpec((2, STEP, *tile), lambda j: (0, high(j), 0, 0)),
            pl.BlockSpec((STEP, *tile), lambda j: (high(j), 0, 0)),
        ),
        scratch_shapes=[
            state, state, state, state,
            pltpu.VMEM((STEP, inputs, lanes), BF16),
            pltpu.VMEM((STEP, inputs, lanes), BF16),
            pltpu.VMEM((lanes // 128 - 1, STEP, *tile), BF16),
        ],
        compiler_params=params(dimension_semantics=("arbitrary",)),
        cost_estimate=pl.CostEstimate(
            flops=8 * flops, bytes_accessed=count * 2 * frames * inputs * 4, transcendentals=0
        ),
        name=f"beamform_{first}",
    )(spectra, cosines, sines)


def place_body(slots, chunks, owner_ref, *refs):
    ins, out_ref, taken = refs[:-2], refs[-2], refs[-1]

    def clear(o, carry):
        taken[o] = 0
        return carry

    lax.fori_loop(0, taken.shape[0], clear, 0)
    base = 0
    for c in range(chunks):
        keep, *rest = ins[c * 5 : c * 5 + 5]
        part = rest[0].shape[1]
        for h in range(2):
            near, far = rest[2 * h], rest[2 * h + 1]

            def body(n, carry, h=h, near=near, far=far, keep=keep, base=base, part=part):
                k = base + h * part + n
                owner = owner_ref[k]
                slot = taken[owner]
                taken[owner] = slot + 1
                total = keep[h * part + n].astype(F32) + near[0, n].astype(F32)
                total = total + far[n].astype(F32)
                out_ref[owner * slots + slot] = total.astype(BF16)
                return carry

            lax.fori_loop(0, part, body, 0, unroll=8)
        base += 2 * part


def place(beam_owner, groups, owner_count, slots):
    flat = [a for g in groups for a in g]
    tile = groups[0][0].shape[1:]

    def first_of(a):
        shape = (1, *a.shape[1:]) if a.ndim == 4 else a.shape
        return pl.BlockSpec(shape, lambda g: (0,) * len(shape))

    return pl.pallas_call(
        functools.partial(place_body, slots, len(groups)),
        grid=(1,),
        out_shape=jax.ShapeDtypeStruct((owner_count * slots, *tile), BF16),
        in_specs=[smem()] + [first_of(a) for a in flat],
        out_specs=pl.BlockSpec((owner_count * slots, *tile), lambda g: (0, 0, 0)),
        scratch_shapes=[pltpu.SMEM((owner_count,), jnp.int32)],
        compiler_params=params(),
        name="place_beams",
    )(beam_owner, *flat)


def deliver_body(live_ref, x_ref, o_ref):
    sources, each, frames, lanes = x_ref.shape
    for s in range(each):
        slot = pl.program_id(0) * each + s

        @pl.when(slot < live_ref[0])
        def _():
            o_ref[s] = x_ref[:, s].astype(F32).reshape(sources * frames, lanes)

        @pl.when(slot >= live_ref[0])
        def _():
            o_ref[s] = jnp.zeros((sources * frames, lanes), F32)


def deliver(live, arrived, sources, slots):
    _, frames, lanes = arrived.shape
    each = 4
    return pl.pallas_call(
        deliver_body,
        grid=(slots // each,),
        out_shape=jax.ShapeDtypeStruct((slots, sources * frames, lanes), F32),
        in_specs=[
            smem(),
            pl.BlockSpec((sources, each, frames, lanes), lambda s: (0, s, 0, 0)),
        ],
        out_specs=pl.BlockSpec((each, sources * frames, lanes), lambda s: (s, 0, 0)),
        compiler_params=params(dimension_semantics=("arbitrary",)),
        name="deliver_beams",
    )(live, arrived.reshape(sources, slots, frames, lanes))


def gram_body(scale, groups, live_ref, x_ref, o_ref):
    slot, row = pl.program_id(0), pl.program_id(1)
    sources, _, _, frames, inputs = x_ref.shape
    each = sources // groups
    depth = each * frames
    over = (((0,), (0,)), ((), ()))

    @pl.when(slot < live_ref[0])
    def _():
        mine = pl.ds(row * each, each)
        r_a = x_ref[mine, 0, 0].reshape(depth, inputs)
        m_a = x_ref[mine, 0, 1].reshape(depth, inputs)
        left_re = jnp.concatenate([r_a, m_a], axis=0)
        left_im = jnp.concatenate([m_a, -r_a], axis=0)
        for b in range(groups):
            r_b = x_ref[b * each : b * each + each, 0, 0].reshape(depth, inputs)
            m_b = x_ref[b * each : b * each + each, 0, 1].reshape(depth, inputs)
            right = jnp.concatenate([r_b, m_b], axis=0)
            cols = pl.ds(b * inputs, inputs)
            re = lax.dot_general(left_re, right, over, preferred_element_type=F32)
            im = lax.dot_general(left_im, right, over, preferred_element_type=F32)
            o_ref[0, 0, :, cols] = re * scale
            o_ref[0, 1, :, cols] = im * scale

    @pl.when(slot >= live_ref[0])
    def _():
        o_ref[...] = jnp.zeros_like(o_ref)


def gram(live, arrived, groups, sources, slots):
    _, _, frames, inputs = arrived.shape
    total = groups * inputs
    scale = 1.0 / (sources // groups * frames)
    return pl.pallas_call(
        functools.partial(gram_body, scale, groups),
        grid=(slots, groups),
        out_shape=jax.ShapeDtypeStruct((slots, 2, total, total), F32),
        in_specs=[
            smem(),
            pl.BlockSpec((sources, 1, 2, frames, inputs), lambda s, a: (0, s, 0, 0, 0)),
        ],
        out_specs=pl.BlockSpec((1, 2, inputs, total), lambda s, a: (s, 0, a, 0)),
        compiler_params=params(dimension_semantics=("arbitrary", "arbitrary")),
        cost_estimate=pl.CostEstimate(
            flops=slots * 8 * total * total * (sources // groups) * frames,
            bytes_accessed=slots * 12 * total * total,
            transcendentals=0,
        ),
        name="gram",
    )(live, arrived.reshape(sources, slots, 2, frames, inputs))


def shards(samples, gram_owner, beam_owner, delays, sections):
    input_count, frame_count, length_total = samples.shape
    half_count = length_total // 2
    inp_count = lax.axis_size("inp")
    chan_count = lax.axis_size("chan")
    inp_here = lax.axis_index("inp")
    chan_here = lax.axis_index("chan")
    owner_count = inp_count * chan_count
    gram_slots = 2 * gram_owner.shape[0] // owner_count
    beam_slots = 2 * half_count // chan_count
    section_width = delays.shape[0] // inp_count

    outgoing, spectra = channelize(samples, gram_owner, owner_count, gram_slots)
    arrived = lax.all_to_all(outgoing, ("inp", "chan"), split_axis=0, concat_axis=0, tiled=True)

    cosines, sines = phases(
        inp_here, sections, delays, input_count, section_width, 2.0 * math.pi / length_total
    )

    side = [(z, z ^ 1) for z in range(inp_count)]
    back = [(z, 3 - z) for z in range(inp_count)]
    chunk = half_count // 2
    groups = []
    for first in range(0, half_count, chunk):
        keep, a, a2, b, b2 = beamform(spectra, cosines, sines, first, chunk)
        a_in = lax.ppermute(a, "inp", side)
        b_in = lax.ppermute(b, "inp", back)
        a_sum = (a2.astype(F32) + a_in[1].astype(F32)).astype(BF16)
        b_sum = (b2.astype(F32) + b_in[1].astype(F32)).astype(BF16)
        a_far = lax.ppermute(a_sum, "inp", back)
        b_far = lax.ppermute(b_sum, "inp", side)
        groups.append((keep, a_in, a_far, b_in, b_far))
    leaving = place(beam_owner, groups, chan_count, beam_slots)
    leaving, arrived = lax.optimization_barrier((leaving, arrived))
    beams_in = lax.all_to_all(leaving, "chan", split_axis=0, concat_axis=0, tiled=True)

    here = inp_here * chan_count + chan_here
    gram_live = jnp.sum((gram_owner == here).astype(jnp.int32)).reshape(1)
    beam_live = jnp.sum((beam_owner == chan_here).astype(jnp.int32)).reshape(1)
    visibilities = gram(gram_live, arrived, inp_count, owner_count, gram_slots)
    formed = deliver(beam_live, beams_in, chan_count, beam_slots)
    return (visibilities, formed[:, None])


def solution(mesh):
    return jax.shard_map(
        shards,
        mesh=mesh,
        in_specs=(P("inp", "chan", None), P(), P(), P(), P()),
        out_specs=(P(("inp", "chan"), None, None, None), P("chan", "inp", None, None)),
        check_vma=False,
    )
```

```python
import functools
import math

import jax
import jax.numpy as jnp
import ml_dtypes
import numpy as np
from jax import lax
from jax.experimental import pallas as pl
from jax.experimental.pallas import tpu as pltpu
from jax.sharding import PartitionSpec as P

BF16 = jnp.bfloat16
F32 = jnp.float32
VMEM_LIMIT = 56 * 1024 * 1024


def fourier_table(length_total):
    half_count = length_total // 2
    rows = np.arange(half_count, dtype=np.int32)
    cols = np.arange(length_total, dtype=np.int32)
    turns = (rows[:, None] * cols[None, :] % length_total).astype(np.float32)
    turns = turns * np.float32(2.0 * math.pi / length_total)
    factor = np.float32(1.0 / math.sqrt(length_total))
    both = np.stack([np.cos(turns) * factor, -np.sin(turns) * factor], axis=1)
    return both.reshape(length_total, length_total).astype(ml_dtypes.bfloat16)


def frame_major(frames):
    count = frames * frames
    matrix = np.zeros((count, count), np.float32)
    for f in range(frames):
        for i in range(frames):
            matrix[f * frames + i, i * frames + f] = 1.0
    return matrix.astype(ml_dtypes.bfloat16)


def params(**more):
    return pltpu.CompilerParams(vmem_limit_bytes=VMEM_LIMIT, **more)


def vmem():
    return pl.BlockSpec(memory_space=pltpu.VMEM)


def smem():
    return pl.BlockSpec(memory_space=pltpu.SMEM)


CHUNKS = 4
PIECE = 32


def channelize_body(
    slots, groups, owner_ref, inp_ref, x_hbm, table_ref, perm_ref, gram_hbm, more_hbm, spec_hbm,
    x_ref, xs, rows, spec, taken, in_sem, gram_sem, spec_sem,
):
    frames, inputs, width = xs.shape
    channels = spec.shape[0]
    gram_channels = owner_ref.shape[0]
    group = frames * frames
    piece = inputs * frames // CHUNKS
    loads = []
    for c in range(CHUNKS):
        part = pl.ds(c * piece, piece)
        loads.append(pltpu.make_async_copy(x_hbm.at[part], x_ref.at[part], in_sem.at[c]))
        loads[-1].start()

    def clear(o, carry):
        taken[o] = 0
        return carry

    lax.fori_loop(0, taken.shape[0], clear, 0)

    def reorder(b, carry):
        block = x_ref[pl.ds(pl.multiple_of(b * group, group), group), :]
        moved = jnp.dot(perm_ref[...], block, preferred_element_type=F32)
        moved = moved.astype(BF16).reshape(frames, frames, width)
        xs[:, pl.ds(pl.multiple_of(b * frames, frames), frames), :] = moved
        return carry

    blocks = piece // group
    for c in range(CHUNKS):
        loads[c].wait()
        lax.fori_loop(c * blocks, (c + 1) * blocks, reorder, 0, unroll=True)

    def fetch(k):
        start = pl.multiple_of(k * 2 * frames, 2 * frames)
        both = [rows[h, pl.ds(start, 2 * frames), :] for h in range(inputs // 128)]
        return jnp.concatenate(both, axis=1).astype(BF16).reshape(2, frames, inputs)

    def low(k, carry):
        owner = owner_ref[k]
        slot = taken[owner]
        taken[owner] = slot + 1
        spec[k] = fetch(k)

        @pl.when(slot == 0)
        def _():
            pltpu.make_async_copy(spec.at[k], gram_hbm.at[owner], gram_sem).start()

        @pl.when(slot > 0)
        def _():
            chans = taken.shape[0] // groups
            ahead = lax.rem(lax.div(owner, chans) - inp_ref[0] + groups, groups)
            at = (lax.rem(owner, chans) * groups + ahead) * (slots - 1) + slot - 1
            pltpu.make_async_copy(spec.at[k], more_hbm.at[at], gram_sem).start()

        return carry

    def high(k, carry):
        spec[k] = fetch(k)
        return carry

    saves = []
    for start in range(0, channels, gram_channels):
        count = min(gram_channels, channels - start)

        def transform(f, carry, start=start, count=count):
            out = lax.dot_general(
                table_ref[2 * start : 2 * (start + count)],
                xs[f],
                (((1,), (1,)), ((), ())),
                preferred_element_type=F32,
            )
            for h in range(inputs // 128):
                at = pl.ds(f + 2 * start * frames, 2 * count, stride=frames)
                rows[h, at, :] = out[:, h * 128 : h * 128 + 128]
            return carry

        lax.fori_loop(0, frames, transform, 0, unroll=4)
        for k in range(start, start + count, PIECE):
            lax.fori_loop(k, k + PIECE, high if start else low, 0, unroll=4)
            part = pl.ds(k, PIECE)
            saves.append(pltpu.make_async_copy(spec.at[part], spec_hbm.at[part], spec_sem.at[k // PIECE]))
            saves[-1].start()
    all_low = pl.ds(0, gram_channels)
    pltpu.make_async_copy(spec.at[all_low], gram_hbm.at[all_low], gram_sem).wait()
    for save in saves:
        save.wait()


def channelize(samples, gram_owner, inp_here, owner_count, groups, slots):
    inputs, frames, width = samples.shape
    channels = width // 2
    anywhere = pl.BlockSpec(memory_space=pl.ANY)
    return pl.pallas_call(
        functools.partial(channelize_body, slots, groups),
        out_shape=(
            jax.ShapeDtypeStruct((owner_count, 2, frames, inputs), BF16),
            jax.ShapeDtypeStruct((owner_count * (slots - 1), 2, frames, inputs), BF16),
            jax.ShapeDtypeStruct((channels, 2, frames, inputs), BF16),
        ),
        in_specs=[smem(), smem(), anywhere, vmem(), vmem()],
        out_specs=(anywhere, anywhere, anywhere),
        scratch_shapes=[
            pltpu.VMEM((inputs * frames, width), BF16),
            pltpu.VMEM((frames, inputs, width), BF16),
            pltpu.VMEM((inputs // 128, 2 * channels * frames, 128), F32),
            pltpu.VMEM((channels, 2, frames, inputs), BF16),
            pltpu.SMEM((owner_count,), jnp.int32),
            pltpu.SemaphoreType.DMA((CHUNKS,)),
            pltpu.SemaphoreType.DMA(()),
            pltpu.SemaphoreType.DMA((channels // PIECE,)),
        ],
        compiler_params=params(),
        name="channelize",
    )(
        gram_owner,
        inp_here.reshape(1),
        samples.reshape(inputs * frames, width),
        jnp.asarray(fourier_table(width)),
        jnp.asarray(frame_major(frames)),
    )


def small_turn(angle):
    square = angle * angle
    cosine = sine = jnp.zeros_like(angle)
    for n in range(6, 0, -1):
        cosine = (cosine + (-1.0) ** n / math.factorial(2 * n)) * square
        sine = (sine + (-1.0) ** n / math.factorial(2 * n + 1)) * square
    return 1.0 + cosine, angle + angle * sine


def phase_body(
    factor, half, inp_ref, section_ref, delay_ref, cos_ref, sin_ref, turned
):
    here = inp_ref[0]
    near = jnp.bitwise_xor(here, 1)
    for q, device in enumerate((here, near, 3 - here, 3 - near)):

        def row(t, carry, q=q, device=device):
            beam = section_ref[device * half + t]
            turned[pl.ds(q * half + t, 1), :] = delay_ref[pl.ds(beam, 1), :]
            return carry

        lax.fori_loop(0, half, row, 0, unroll=8)
    for q in range(turned.shape[0] // half):
        cosines, sines = small_turn(turned[q * half : q * half + half] * factor)
        for source, target in ((cosines, cos_ref), (sines, sin_ref)):
            rows = jnp.concatenate([source, source], axis=0).T
            target[:, q * 2 * half : (q + 1) * 2 * half] = rows


def phases(inp_here, sections, delays, inputs, half, factor):
    beams = delays.shape[0]
    return pl.pallas_call(
        functools.partial(phase_body, factor, half),
        grid_spec=pltpu.PrefetchScalarGridSpec(
            num_scalar_prefetch=2,
            grid=(1,),
            in_specs=[pl.BlockSpec((beams, inputs), lambda g, inp, *_: (0, inp[0]))],
            out_specs=[
                pl.BlockSpec((inputs, 2 * beams), lambda g, *_: (0, 0)),
                pl.BlockSpec((inputs, 2 * beams), lambda g, *_: (0, 0)),
            ],
            scratch_shapes=[pltpu.VMEM((beams, inputs), F32)],
        ),
        out_shape=[jax.ShapeDtypeStruct((inputs, 2 * beams), F32)] * 2,
        compiler_params=params(),
        name="phases",
    )(inp_here.reshape(1), sections, delays)


STEP = 16
CHANNEL_CHUNKS = ((0, 128), (128, 128))


def turn(a, b, c, s):
    return a * c - b * s, b * c + a * s


def beam_body(
    first, half, spec_ref, cos_ref, sin_ref, keep_ref, a_ref, a2_ref, b_ref, b2_ref,
    big_c, big_s, now_c, now_s, even, odd, stage,
):
    step = pl.program_id(0)
    last = pl.num_programs(0) - 1
    inputs, lanes = cos_ref.shape
    frames = keep_ref.shape[1]
    tiles = lanes // 128

    @pl.when(step == 0)
    def _():
        def start(r, carry):
            rows = pl.ds(pl.multiple_of(r * 16, 16), 16)
            for t in range(tiles):
                cols = pl.ds(t * 128, 128)
                c, s = cos_ref[rows, cols], sin_ref[rows, cols]
                done = 1
                while done < STEP // 2:
                    c, s = turn(c, s, c, s)
                    done *= 2
                mid = c, s
                c, s = turn(c, s, c, s)
                done *= 2
                big_c[rows, cols] = c
                big_s[rows, cols] = s
                while done <= first:
                    if first & done:
                        mid = turn(*mid, c, s)
                    c, s = turn(c, s, c, s)
                    done *= 2
                c, s = mid
                lane = lax.broadcasted_iota(jnp.int32, c.shape, 1)
                scale = 1.0 / 32.0
                now_c[rows, cols] = jnp.where(lane < half, c, -s) * scale
                now_s[rows, cols] = jnp.where(lane < half, s, c) * scale
            return carry

        lax.fori_loop(0, inputs // 16, start, 0)

    def make(r, weights):
        rows = pl.ds(pl.multiple_of(r * 16, 16), 16)
        a, b = now_c[rows], now_s[rows]
        c1, s1 = cos_ref[rows], sin_ref[rows]
        twice = c1 + c1
        p, q = a * c1, b * s1
        below, above = (a, p + q), (a, p - q)
        mid = STEP // 2
        weights[mid, rows] = a.astype(BF16)
        for m in range(1, mid + 1):
            weights[mid - m, rows] = below[1].astype(BF16)
            if m < mid:
                weights[mid + m, rows] = above[1].astype(BF16)
                below = below[1], twice * below[1] - below[0]
                above = above[1], twice * above[1] - above[0]
        now_c[rows], now_s[rows] = turn(a, b, big_c[rows], big_s[rows])

    lane = lax.broadcasted_iota(jnp.int32, (frames, 128), 1)
    sign = jnp.where(lane < half, -1.0, 1.0).astype(F32)

    def form(m, weights):
        got = jnp.dot(spec_ref[m], weights[m], preferred_element_type=F32)
        parts = []
        for t in range(tiles):
            real = got[:frames, t * 128 : t * 128 + 128]
            imag = got[frames:, t * 128 : t * 128 + 128]
            parts.append((real + sign * pltpu.roll(imag, half, 1)).astype(BF16))
        keep_ref[m] = parts[0]
        for t in range(1, tiles):
            stage[t - 1, m] = parts[t]

    @pl.when(step == 0)
    def _():
        @pl.loop(0, inputs // 16, unroll=2)
        def _(r):
            make(r, even)

    @pl.when((step > 0) & (step < last) & (step % 2 == 1))
    def _():
        @pl.loop(0, STEP, unroll=True)
        def _(r):
            form(r, even)
            make(r, odd)

    @pl.when((step > 0) & (step < last) & (step % 2 == 0))
    def _():
        @pl.loop(0, STEP, unroll=True)
        def _(r):
            form(r, odd)
            make(r, even)

    @pl.when(step == last)
    def _():
        @pl.loop(0, STEP, unroll=True)
        def _(r):
            form(r, odd)

    middle = last // 2

    @pl.when((step > 0) & (step <= middle))
    def _():
        a_ref[0], a_ref[1], a2_ref[...] = stage[0], stage[2], stage[1]

    @pl.when(step > middle)
    def _():
        b_ref[0], b_ref[1], b2_ref[...] = stage[1], stage[2], stage[0]


def beamform(spectra, cosines, sines, first, count):
    channels, _, frames, inputs = spectra.shape
    lanes = cosines.shape[1]
    part = count // 2
    tile = (frames, 128)
    steps = count // STEP
    assert steps % 2 == 0 and inputs // 16 == STEP
    spectra = spectra.reshape(channels, 2 * frames, inputs)
    state = pltpu.VMEM((inputs, lanes), F32)
    at = lambda j: jnp.maximum(j - 1, 0)
    low = lambda j: jnp.minimum(at(j), steps // 2 - 1)
    high = lambda j: jnp.maximum(at(j) - steps // 2, 0)
    whole = lambda *shape: pl.BlockSpec(shape, lambda j: (0,) * len(shape))
    flops = count * 2 * (2 * frames) * inputs * lanes
    return pl.pallas_call(
        functools.partial(beam_body, first, 64),
        grid=(steps + 1,),
        out_shape=(
            jax.ShapeDtypeStruct((count, *tile), BF16),
            jax.ShapeDtypeStruct((2, part, *tile), BF16),
            jax.ShapeDtypeStruct((part, *tile), BF16),
            jax.ShapeDtypeStruct((2, part, *tile), BF16),
            jax.ShapeDtypeStruct((part, *tile), BF16),
        ),
        in_specs=[
            pl.BlockSpec((STEP, 2 * frames, inputs), lambda j: (first // STEP + at(j), 0, 0)),
            whole(inputs, lanes),
            whole(inputs, lanes),
        ],
        out_specs=(
            pl.BlockSpec((STEP, *tile), lambda j: (at(j), 0, 0)),
            pl.BlockSpec((2, STEP, *tile), lambda j: (0, low(j), 0, 0)),
            pl.BlockSpec((STEP, *tile), lambda j: (low(j), 0, 0)),
            pl.BlockSpec((2, STEP, *tile), lambda j: (0, high(j), 0, 0)),
            pl.BlockSpec((STEP, *tile), lambda j: (high(j), 0, 0)),
        ),
        scratch_shapes=[
            state, state, state, state,
            pltpu.VMEM((STEP, inputs, lanes), BF16),
            pltpu.VMEM((STEP, inputs, lanes), BF16),
            pltpu.VMEM((lanes // 128 - 1, STEP, *tile), BF16),
        ],
        compiler_params=params(dimension_semantics=("arbitrary",)),
        cost_estimate=pl.CostEstimate(
            flops=8 * flops, bytes_accessed=count * 2 * frames * inputs * 4, transcendentals=0
        ),
        name=f"beamform_{first}",
    )(spectra, cosines, sines)


def place_body(first, slots, owner_ref, keep, a_near, a_far, b_near, b_far, *rest):
    out_hbm, total, taken, sem = rest[-4:]
    part = a_far.shape[0]

    def clear(o, carry):
        taken[o] = 0
        return carry

    lax.fori_loop(0, taken.shape[0], clear, 0, unroll=8)

    def count(k, carry):
        taken[owner_ref[k]] = taken[owner_ref[k]] + 1
        return carry

    if first:
        lax.fori_loop(0, first, count, 0, unroll=8)
    for h, (near, far) in enumerate(((a_near, a_far), (b_near, b_far))):

        def body(n, carry, h=h, near=near, far=far):
            k = h * part + n
            owner = owner_ref[first + k]
            slot = taken[owner]
            taken[owner] = slot + 1
            value = keep[k].astype(F32) + near[0, n].astype(F32) + far[n].astype(F32)
            total[k] = value.astype(BF16)
            pltpu.make_async_copy(total.at[k], out_hbm.at[owner * slots + slot], sem).start()
            return carry

        lax.fori_loop(0, part, body, 0, unroll=8)
    pltpu.make_async_copy(total, out_hbm.at[pl.ds(0, 2 * part)], sem).wait()


def place(beam_owner, first, group, owner_count, slots, before):
    tile = group[0].shape[1:]
    count = group[0].shape[0]
    anywhere = pl.BlockSpec(memory_space=pl.ANY)

    def first_of(a):
        shape = (1, *a.shape[1:]) if a.ndim == 4 else a.shape
        return pl.BlockSpec(shape, lambda g: (0,) * len(shape))

    more = [] if before is None else [before]
    return pl.pallas_call(
        functools.partial(place_body, first, slots),
        grid=(1,),
        out_shape=jax.ShapeDtypeStruct((owner_count * slots, *tile), BF16),
        in_specs=[smem()] + [first_of(a) for a in group] + [anywhere] * len(more),
        out_specs=anywhere,
        scratch_shapes=[
            pltpu.VMEM((count, *tile), BF16),
            pltpu.SMEM((owner_count,), jnp.int32),
            pltpu.SemaphoreType.DMA(()),
        ],
        input_output_aliases={6: 0} if more else {},
        compiler_params=params(),
        name=f"place_beams_{first}",
    )(beam_owner, *group, *more)


def deliver_body(live_ref, x_ref, o_ref):
    sources, each, frames, lanes = x_ref.shape
    for s in range(each):
        slot = pl.program_id(0) * each + s

        @pl.when(slot < live_ref[0])
        def _():
            o_ref[s] = x_ref[:, s].astype(F32).reshape(sources * frames, lanes)

        @pl.when(slot >= live_ref[0])
        def _():
            o_ref[s] = jnp.zeros((sources * frames, lanes), F32)


def deliver(live, arrived, sources, slots):
    _, frames, lanes = arrived.shape
    each = 4
    return pl.pallas_call(
        deliver_body,
        grid=(slots // each,),
        out_shape=jax.ShapeDtypeStruct((slots, sources * frames, lanes), F32),
        in_specs=[
            smem(),
            pl.BlockSpec((sources, each, frames, lanes), lambda s: (0, s, 0, 0)),
        ],
        out_specs=pl.BlockSpec((each, sources * frames, lanes), lambda s: (s, 0, 0)),
        compiler_params=params(dimension_semantics=("arbitrary",)),
        name="deliver_beams",
    )(live, arrived.reshape(sources, slots, frames, lanes))


def gram_body(scale, slot, blocks, here_ref, live_ref, *refs):
    ins, o_ref, xs = refs[:blocks], refs[-2], refs[-1]
    row = pl.program_id(0)
    groups, _, depth, inputs = xs.shape
    over = (((0,), (0,)), ((), ()))

    @pl.when(live_ref[0] > slot)
    def _():
        @pl.when(row == 0)
        def _():
            for n, ref in enumerate(ins):
                parts = groups // blocks
                value = ref[...].reshape(parts, -1, 2, *ref.shape[-2:])
                for d in range(parts):
                    for p in range(2):
                        xs[n * parts + d, p] = value[d, :, p].reshape(depth, inputs)

        r_a, m_a = xs[row, 0], xs[row, 1]
        left_re = jnp.concatenate([r_a, m_a], axis=0)
        left_im = jnp.concatenate([m_a, -r_a], axis=0)
        for d in range(groups):
            right = xs[d].reshape(2 * depth, inputs)
            block = lax.rem(here_ref[0] - d + groups, groups) if blocks > 1 else d
            cols = pl.ds(pl.multiple_of(block * inputs, inputs), inputs)
            re = lax.dot_general(left_re, right, over, preferred_element_type=F32)
            im = lax.dot_general(left_im, right, over, preferred_element_type=F32)
            o_ref[0, 0, :, cols] = re * scale
            o_ref[0, 1, :, cols] = im * scale

    @pl.when(live_ref[0] <= slot)
    def _():
        o_ref[...] = jnp.zeros_like(o_ref)


def gram(here, live, arrays, groups, slot, slots, before):
    frames, inputs = arrays[-1].shape[-2:]
    total = groups * inputs
    blocks = len(arrays)
    depth = arrays[-1].shape[0] * frames * blocks // groups
    back = lambda a, here: lax.rem(here[0] - a + groups, groups) if blocks > 1 else a
    whole = lambda x: pl.BlockSpec(x.shape, lambda a, *_: (0,) * x.ndim)
    first = [whole(arrays[0])]
    if blocks > 1:
        chans, _, _, *rest = arrays[0].shape
        first = [pl.BlockSpec((chans, 1, 1, *rest), lambda a, *_: (0, 0, slot - 1, 0, 0, 0))]
    more = [] if before is None else [before]
    return pl.pallas_call(
        functools.partial(gram_body, 1.0 / depth, slot, blocks),
        grid_spec=pltpu.PrefetchScalarGridSpec(
            num_scalar_prefetch=2,
            grid=(groups,),
            in_specs=first
            + [whole(x) for x in arrays[1:]]
            + [pl.BlockSpec(memory_space=pl.ANY)] * len(more),
            out_specs=pl.BlockSpec(
                (1, 2, inputs, total), lambda a, here, live: (slot, 0, back(a, here), 0)
            ),
            scratch_shapes=[pltpu.VMEM((groups, 2, depth, inputs), BF16)],
        ),
        out_shape=jax.ShapeDtypeStruct((slots, 2, total, total), F32),
        input_output_aliases={2 + blocks: 0} if more else {},
        compiler_params=params(dimension_semantics=("arbitrary",)),
        cost_estimate=pl.CostEstimate(
            flops=8 * total * total * depth, bytes_accessed=12 * total * total, transcendentals=0
        ),
        name=f"gram_{slot}",
    )(here, live, *arrays, *more)


def shards(samples, gram_owner, beam_owner, delays, sections):
    input_count, frame_count, length_total = samples.shape
    half_count = length_total // 2
    inp_count = lax.axis_size("inp")
    chan_count = lax.axis_size("chan")
    inp_here = lax.axis_index("inp")
    chan_here = lax.axis_index("chan")
    owner_count = inp_count * chan_count
    gram_slots = 2 * gram_owner.shape[0] // owner_count
    beam_slots = 2 * half_count // chan_count
    section_width = delays.shape[0] // inp_count

    outgoing, later, spectra = channelize(
        samples, gram_owner, inp_here, owner_count, inp_count, gram_slots
    )
    arrived = lax.all_to_all(outgoing, ("inp", "chan"), split_axis=0, concat_axis=0, tiled=True)

    cosines, sines = phases(
        inp_here, sections, delays, input_count, section_width, 2.0 * math.pi / length_total
    )

    side = [(z, z ^ 1) for z in range(inp_count)]
    back = [(z, 3 - z) for z in range(inp_count)]
    parts = []
    near = []
    for first, count in CHANNEL_CHUNKS:
        keep, a, a2, b, b2 = beamform(spectra, cosines, sines, first, count)
        spectra, keep = lax.optimization_barrier((spectra, keep))
        parts.append((keep, a, a2, b, b2))
        if first + count < half_count:
            near.append((lax.ppermute(a, "inp", side), lax.ppermute(b, "inp", back)))
    later, arrived, parts, near = lax.optimization_barrier((later, arrived, parts, near))
    later = lax.all_to_all(later, "chan", split_axis=0, concat_axis=0, tiled=True)
    later = later.reshape(chan_count, inp_count, gram_slots - 1, *later.shape[1:])
    near.append((lax.ppermute(parts[-1][1], "inp", side), lax.ppermute(parts[-1][3], "inp", back)))
    far = []
    for n, (_, _, a2, _, b2) in enumerate(parts):
        a_in, b_in = near[n]
        if far:
            a_in, b_in, far[-1] = lax.optimization_barrier((a_in, b_in, far[-1]))
        a_sum = (a2.astype(F32) + a_in[1].astype(F32)).astype(BF16)
        b_sum = (b2.astype(F32) + b_in[1].astype(F32)).astype(BF16)
        far.append((lax.ppermute(a_sum, "inp", back), lax.ppermute(b_sum, "inp", side)))
        near[n] = (a_in, b_in)
    leaving = None
    for (first, _), (keep, *_), (a_in, b_in), (a_far, b_far) in zip(CHANNEL_CHUNKS, parts, near, far):
        group = (keep, a_in, a_far, b_in, b_far)
        leaving = place(beam_owner, first, group, chan_count, beam_slots, leaving)
    leaving, later = lax.optimization_barrier((leaving, later))
    beams_in = lax.all_to_all(leaving, "chan", split_axis=0, concat_axis=0, tiled=True)

    here = inp_here * chan_count + chan_here
    gram_live = jnp.sum((gram_owner == here).astype(jnp.int32)).reshape(1)
    beam_live = jnp.sum((beam_owner == chan_here).astype(jnp.int32)).reshape(1)
    at = inp_here.reshape(1)
    visibilities = gram(at, gram_live, [arrived], inp_count, 0, gram_slots, None)
    for slot in range(1, gram_slots):
        moved = [
            lax.ppermute(later[:, d, slot - 1], "inp", [(z, (z + d) % inp_count) for z in range(inp_count)])
            for d in range(1, inp_count)
        ]
        visibilities = gram(
            at, gram_live, [later, *moved], inp_count, slot, gram_slots, visibilities
        )
    formed = deliver(beam_live, beams_in, chan_count, beam_slots)
    return (visibilities, formed[:, None])


def solution(mesh):
    return jax.shard_map(
        shards,
        mesh=mesh,
        in_specs=(P("inp", "chan", None), P(), P(), P(), P()),
        out_specs=(P(("inp", "chan"), None, None, None), P("chan", "inp", None, None)),
        check_vma=False,
    )
```

```python
import functools
import math

import jax
import jax.numpy as jnp
import ml_dtypes
import numpy as np
from jax import lax
from jax.experimental import pallas as pl
from jax.experimental.pallas import tpu as pltpu
from jax.sharding import PartitionSpec as P

BF16 = jnp.bfloat16
F32 = jnp.float32
VMEM_LIMIT = 56 * 1024 * 1024


def fourier_table(length_total):
    half_count = length_total // 2
    rows = np.arange(half_count, dtype=np.int32)
    cols = np.arange(length_total, dtype=np.int32)
    turns = (rows[:, None] * cols[None, :] % length_total).astype(np.float32)
    turns = turns * np.float32(2.0 * math.pi / length_total)
    factor = np.float32(1.0 / math.sqrt(length_total))
    both = np.stack([np.cos(turns) * factor, -np.sin(turns) * factor], axis=1)
    return both.reshape(length_total, length_total).astype(ml_dtypes.bfloat16)


def frame_major(frames):
    count = frames * frames
    matrix = np.zeros((count, count), np.float32)
    for f in range(frames):
        for i in range(frames):
            matrix[f * frames + i, i * frames + f] = 1.0
    return matrix.astype(ml_dtypes.bfloat16)


def params(**more):
    return pltpu.CompilerParams(vmem_limit_bytes=VMEM_LIMIT, **more)


def vmem():
    return pl.BlockSpec(memory_space=pltpu.VMEM)


def smem():
    return pl.BlockSpec(memory_space=pltpu.SMEM)


CHUNKS = 4
PIECE = 32


def channelize_body(
    groups, owner_ref, inp_ref, x_hbm, table_ref, perm_ref, gram_hbm, more_hbm, spec_hbm,
    x_ref, xs, rows, spec, taken, in_sem, gram_sem, spec_sem,
):
    frames, inputs, width = xs.shape
    channels = spec.shape[0]
    gram_channels = owner_ref.shape[0]
    group = frames * frames
    piece = inputs * frames // CHUNKS
    loads = []
    for c in range(CHUNKS):
        part = pl.ds(c * piece, piece)
        loads.append(pltpu.make_async_copy(x_hbm.at[part], x_ref.at[part], in_sem.at[c]))
        loads[-1].start()

    def clear(o, carry):
        taken[o] = 0
        return carry

    lax.fori_loop(0, taken.shape[0], clear, 0)

    def reorder(b, carry):
        block = x_ref[pl.ds(pl.multiple_of(b * group, group), group), :]
        moved = jnp.dot(perm_ref[...], block, preferred_element_type=F32)
        moved = moved.astype(BF16).reshape(frames, frames, width)
        xs[:, pl.ds(pl.multiple_of(b * frames, frames), frames), :] = moved
        return carry

    blocks = piece // group
    for c in range(CHUNKS):
        loads[c].wait()
        lax.fori_loop(c * blocks, (c + 1) * blocks, reorder, 0, unroll=True)

    def fetch(k):
        start = pl.multiple_of(k * 2 * frames, 2 * frames)
        both = [rows[h, pl.ds(start, 2 * frames), :] for h in range(inputs // 128)]
        return jnp.concatenate(both, axis=1).astype(BF16).reshape(2, frames, inputs)

    def low(k, carry):
        owner = owner_ref[k]
        slot = taken[owner]
        taken[owner] = slot + 1
        spec[k] = fetch(k)

        @pl.when(slot == 0)
        def _():
            both = gram_hbm.at[owner, pl.ds(0, 2)]
            pltpu.make_async_copy(spec.at[k], both, gram_sem).start()

        @pl.when(slot > 0)
        def _():
            chans = taken.shape[0] // groups
            ahead = lax.rem(lax.div(owner, chans) - inp_ref[0] + groups, groups)
            at = lax.rem(owner, chans) * groups + ahead
            pltpu.make_async_copy(spec.at[k, 0], gram_hbm.at[owner, 2], gram_sem).start()
            pltpu.make_async_copy(spec.at[k, 1], more_hbm.at[at], gram_sem).start()

        return carry

    def high(k, carry):
        spec[k] = fetch(k)
        return carry

    saves = []
    for start in range(0, channels, gram_channels):
        count = min(gram_channels, channels - start)

        def transform(f, carry, start=start, count=count):
            out = lax.dot_general(
                table_ref[2 * start : 2 * (start + count)],
                xs[f],
                (((1,), (1,)), ((), ())),
                preferred_element_type=F32,
            )
            for h in range(inputs // 128):
                at = pl.ds(f + 2 * start * frames, 2 * count, stride=frames)
                rows[h, at, :] = out[:, h * 128 : h * 128 + 128]
            return carry

        lax.fori_loop(0, frames, transform, 0, unroll=16)
        for k in range(start, start + count, PIECE):
            lax.fori_loop(k, k + PIECE, high if start else low, 0, unroll=4)
            part = pl.ds(k, PIECE)
            saves.append(pltpu.make_async_copy(spec.at[part], spec_hbm.at[part], spec_sem.at[k // PIECE]))
            saves[-1].start()
    all_low = pl.ds(0, gram_channels)
    pltpu.make_async_copy(spec.at[all_low], spec_hbm.at[all_low], gram_sem).wait()
    for save in saves:
        save.wait()


def channelize(samples, gram_owner, inp_here, owner_count, groups):
    inputs, frames, width = samples.shape
    channels = width // 2
    anywhere = pl.BlockSpec(memory_space=pl.ANY)
    return pl.pallas_call(
        functools.partial(channelize_body, groups),
        out_shape=(
            jax.ShapeDtypeStruct((owner_count, 3, frames, inputs), BF16),
            jax.ShapeDtypeStruct((owner_count, frames, inputs), BF16),
            jax.ShapeDtypeStruct((channels, 2, frames, inputs), BF16),
        ),
        in_specs=[smem(), smem(), anywhere, vmem(), vmem()],
        out_specs=(anywhere, anywhere, anywhere),
        scratch_shapes=[
            pltpu.VMEM((inputs * frames, width), BF16),
            pltpu.VMEM((frames, inputs, width), BF16),
            pltpu.VMEM((inputs // 128, 2 * channels * frames, 128), F32),
            pltpu.VMEM((channels, 2, frames, inputs), BF16),
            pltpu.SMEM((owner_count,), jnp.int32),
            pltpu.SemaphoreType.DMA((CHUNKS,)),
            pltpu.SemaphoreType.DMA(()),
            pltpu.SemaphoreType.DMA((channels // PIECE,)),
        ],
        compiler_params=params(),
        name="channelize",
    )(
        gram_owner,
        inp_here.reshape(1),
        samples.reshape(inputs * frames, width),
        jnp.asarray(fourier_table(width)),
        jnp.asarray(frame_major(frames)),
    )


def small_turn(angle):
    square = angle * angle
    cosine = sine = jnp.zeros_like(angle)
    for n in range(6, 0, -1):
        cosine = (cosine + (-1.0) ** n / math.factorial(2 * n)) * square
        sine = (sine + (-1.0) ** n / math.factorial(2 * n + 1)) * square
    return 1.0 + cosine, angle + angle * sine


def phase_body(
    factor, half, inp_ref, section_ref, delay_ref, cos_ref, sin_ref, turned
):
    here = inp_ref[0]
    near = jnp.bitwise_xor(here, 1)
    for q, device in enumerate((here, near, 3 - here, 3 - near)):

        def row(t, carry, q=q, device=device):
            beam = section_ref[device * half + t]
            turned[pl.ds(q * half + t, 1), :] = delay_ref[pl.ds(beam, 1), :]
            return carry

        lax.fori_loop(0, half, row, 0, unroll=8)
    for q in range(turned.shape[0] // half):
        cosines, sines = small_turn(turned[q * half : q * half + half] * factor)
        for source, target in ((cosines, cos_ref), (sines, sin_ref)):
            rows = jnp.concatenate([source, source], axis=0).T
            target[:, q * 2 * half : (q + 1) * 2 * half] = rows


def phases(inp_here, sections, delays, inputs, half, factor):
    beams = delays.shape[0]
    return pl.pallas_call(
        functools.partial(phase_body, factor, half),
        grid_spec=pltpu.PrefetchScalarGridSpec(
            num_scalar_prefetch=2,
            grid=(1,),
            in_specs=[pl.BlockSpec((beams, inputs), lambda g, inp, *_: (0, inp[0]))],
            out_specs=[
                pl.BlockSpec((inputs, 2 * beams), lambda g, *_: (0, 0)),
                pl.BlockSpec((inputs, 2 * beams), lambda g, *_: (0, 0)),
            ],
            scratch_shapes=[pltpu.VMEM((beams, inputs), F32)],
        ),
        out_shape=[jax.ShapeDtypeStruct((inputs, 2 * beams), F32)] * 2,
        compiler_params=params(),
        name="phases",
    )(inp_here.reshape(1), sections, delays)


STEP = 16
PAIR = 2 * STEP
CHANNEL_CHUNKS = ((0, 128), (128, 128))


def turn(a, b, c, s):
    return a * c - b * s, b * c + a * s


def beam_body(
    first, half, spec_ref, cos_ref, sin_ref, keep_ref, a_ref, a2_ref, b_ref, b2_ref,
    big_c, big_s, now_c, now_s, even, odd, stage,
):
    step = pl.program_id(0)
    last = pl.num_programs(0) - 1
    inputs, lanes = cos_ref.shape
    frames = keep_ref.shape[1]
    tiles = lanes // 128

    @pl.when(step == 0)
    def _():
        def start(r, carry):
            rows = pl.ds(pl.multiple_of(r * 16, 16), 16)
            for t in range(tiles):
                cols = pl.ds(t * 128, 128)
                c, s = cos_ref[rows, cols], sin_ref[rows, cols]
                done = 1
                while done < STEP // 2:
                    c, s = turn(c, s, c, s)
                    done *= 2
                mid = c, s
                c, s = turn(c, s, c, s)
                done *= 2
                big_c[rows, cols] = c
                big_s[rows, cols] = s
                while done <= first:
                    if first & done:
                        mid = turn(*mid, c, s)
                    c, s = turn(c, s, c, s)
                    done *= 2
                c, s = mid
                lane = lax.broadcasted_iota(jnp.int32, c.shape, 1)
                scale = 1.0 / 32.0
                now_c[rows, cols] = jnp.where(lane < half, c, -s) * scale
                now_s[rows, cols] = jnp.where(lane < half, s, c) * scale
            return carry

        lax.fori_loop(0, inputs // 16, start, 0)

    def make(r, weights):
        rows = pl.ds(pl.multiple_of(r * 16, 16), 16)
        a, b = now_c[rows], now_s[rows]
        c1, s1 = cos_ref[rows], sin_ref[rows]
        twice = c1 + c1
        p, q = a * c1, b * s1
        below, above = (a, p + q), (a, p - q)
        mid = STEP // 2
        weights[mid, rows] = a.astype(BF16)
        for m in range(1, mid + 1):
            weights[mid - m, rows] = below[1].astype(BF16)
            if m < mid:
                weights[mid + m, rows] = above[1].astype(BF16)
                below = below[1], twice * below[1] - below[0]
                above = above[1], twice * above[1] - above[0]
        now_c[rows], now_s[rows] = turn(a, b, big_c[rows], big_s[rows])

    lane = lax.broadcasted_iota(jnp.int32, (frames, 128), 1)
    sign = jnp.where(lane < half, -1.0, 1.0).astype(F32)

    def form(m, weights):
        got = jnp.dot(spec_ref[m], weights[m % STEP], preferred_element_type=F32)
        parts = []
        for t in range(tiles):
            real = got[:frames, t * 128 : t * 128 + 128]
            imag = got[frames:, t * 128 : t * 128 + 128]
            parts.append((real + sign * pltpu.roll(imag, half, 1)).astype(BF16))
        keep_ref[m] = parts[0]
        for t in range(1, tiles):
            stage[t - 1, m] = parts[t]

    @pl.when(step == 0)
    def _():
        @pl.loop(0, inputs // 16, unroll=2)
        def _(r):
            make(r, even)

    @pl.when(step > 0)
    def _():
        @pl.loop(0, STEP, unroll=True)
        def _(r):
            form(r, even)
            make(r, odd)

    @pl.when((step > 0) & (step < last))
    def _():
        @pl.loop(0, STEP, unroll=True)
        def _(r):
            form(STEP + r, odd)
            make(r, even)

    @pl.when(step == last)
    def _():
        @pl.loop(0, STEP, unroll=True)
        def _(r):
            form(STEP + r, odd)

    middle = last // 2

    @pl.when((step > 0) & (step <= middle))
    def _():
        a_ref[0], a_ref[1], a2_ref[...] = stage[0], stage[2], stage[1]

    @pl.when(step > middle)
    def _():
        b_ref[0], b_ref[1], b2_ref[...] = stage[1], stage[2], stage[0]


def beamform(spectra, cosines, sines, first, count):
    channels, _, frames, inputs = spectra.shape
    lanes = cosines.shape[1]
    part = count // 2
    tile = (frames, 128)
    steps = count // PAIR
    assert steps % 2 == 0 and inputs // 16 == STEP
    spectra = spectra.reshape(channels, 2 * frames, inputs)
    state = pltpu.VMEM((inputs, lanes), F32)
    at = lambda j: jnp.maximum(j - 1, 0)
    low = lambda j: jnp.minimum(at(j), steps // 2 - 1)
    high = lambda j: jnp.maximum(at(j) - steps // 2, 0)
    whole = lambda *shape: pl.BlockSpec(shape, lambda j: (0,) * len(shape))
    flops = count * 2 * (2 * frames) * inputs * lanes
    return pl.pallas_call(
        functools.partial(beam_body, first, 64),
        grid=(steps + 1,),
        out_shape=(
            jax.ShapeDtypeStruct((count, *tile), BF16),
            jax.ShapeDtypeStruct((2, part, *tile), BF16),
            jax.ShapeDtypeStruct((part, *tile), BF16),
            jax.ShapeDtypeStruct((2, part, *tile), BF16),
            jax.ShapeDtypeStruct((part, *tile), BF16),
        ),
        in_specs=[
            pl.BlockSpec((PAIR, 2 * frames, inputs), lambda j: (first // PAIR + at(j), 0, 0)),
            whole(inputs, lanes),
            whole(inputs, lanes),
        ],
        out_specs=(
            pl.BlockSpec((PAIR, *tile), lambda j: (at(j), 0, 0)),
            pl.BlockSpec((2, PAIR, *tile), lambda j: (0, low(j), 0, 0)),
            pl.BlockSpec((PAIR, *tile), lambda j: (low(j), 0, 0)),
            pl.BlockSpec((2, PAIR, *tile), lambda j: (0, high(j), 0, 0)),
            pl.BlockSpec((PAIR, *tile), lambda j: (high(j), 0, 0)),
        ),
        scratch_shapes=[
            state, state, state, state,
            pltpu.VMEM((STEP, inputs, lanes), BF16),
            pltpu.VMEM((STEP, inputs, lanes), BF16),
            pltpu.VMEM((lanes // 128 - 1, PAIR, *tile), BF16),
        ],
        compiler_params=params(dimension_semantics=("arbitrary",)),
        cost_estimate=pl.CostEstimate(
            flops=8 * flops, bytes_accessed=count * 2 * frames * inputs * 4, transcendentals=0
        ),
        name=f"beamform_{first}",
    )(spectra, cosines, sines)


def place_body(first, slots, owner_ref, keep, a_near, a_far, b_near, b_far, *rest):
    out_hbm, total, taken, sem = rest[-4:]
    part = a_far.shape[0]

    def clear(o, carry):
        taken[o] = 0
        return carry

    lax.fori_loop(0, taken.shape[0], clear, 0, unroll=8)

    def count(k, carry):
        taken[owner_ref[k]] = taken[owner_ref[k]] + 1
        return carry

    if first:
        lax.fori_loop(0, first, count, 0, unroll=8)
    for h, (near, far) in enumerate(((a_near, a_far), (b_near, b_far))):

        def body(n, carry, h=h, near=near, far=far):
            k = h * part + n
            owner = owner_ref[first + k]
            slot = taken[owner]
            taken[owner] = slot + 1
            value = keep[k].astype(F32) + near[0, n].astype(F32) + far[n].astype(F32)
            total[k] = value.astype(BF16)
            pltpu.make_async_copy(total.at[k], out_hbm.at[owner * slots + slot], sem).start()
            return carry

        lax.fori_loop(0, part, body, 0, unroll=8)
    pltpu.make_async_copy(total, out_hbm.at[pl.ds(0, 2 * part)], sem).wait()


def place(beam_owner, first, group, owner_count, slots, before):
    tile = group[0].shape[1:]
    count = group[0].shape[0]
    anywhere = pl.BlockSpec(memory_space=pl.ANY)

    def first_of(a):
        shape = (1, *a.shape[1:]) if a.ndim == 4 else a.shape
        return pl.BlockSpec(shape, lambda g: (0,) * len(shape))

    more = [] if before is None else [before]
    return pl.pallas_call(
        functools.partial(place_body, first, slots),
        grid=(1,),
        out_shape=jax.ShapeDtypeStruct((owner_count * slots, *tile), BF16),
        in_specs=[smem()] + [first_of(a) for a in group] + [anywhere] * len(more),
        out_specs=anywhere,
        scratch_shapes=[
            pltpu.VMEM((count, *tile), BF16),
            pltpu.SMEM((owner_count,), jnp.int32),
            pltpu.SemaphoreType.DMA(()),
        ],
        input_output_aliases={6: 0} if more else {},
        compiler_params=params(),
        name=f"place_beams_{first}",
    )(beam_owner, *group, *more)


def deliver_body(live_ref, x_ref, o_ref):
    sources, each, frames, lanes = x_ref.shape
    for s in range(each):
        slot = pl.program_id(0) * each + s

        @pl.when(slot < live_ref[0])
        def _():
            o_ref[s] = x_ref[:, s].astype(F32).reshape(sources * frames, lanes)

        @pl.when(slot >= live_ref[0])
        def _():
            o_ref[s] = jnp.zeros((sources * frames, lanes), F32)


def deliver(live, arrived, sources, slots):
    _, frames, lanes = arrived.shape
    each = 4
    return pl.pallas_call(
        deliver_body,
        grid=(slots // each,),
        out_shape=jax.ShapeDtypeStruct((slots, sources * frames, lanes), F32),
        in_specs=[
            smem(),
            pl.BlockSpec((sources, each, frames, lanes), lambda s: (0, s, 0, 0)),
        ],
        out_specs=pl.BlockSpec((each, sources * frames, lanes), lambda s: (s, 0, 0)),
        compiler_params=params(dimension_semantics=("arbitrary",)),
        name="deliver_beams",
    )(live, arrived.reshape(sources, slots, frames, lanes))


def gram_body(scale, slot, here_ref, live_ref, direct_ref, *refs):
    others, o_ref, xs = refs[:4], refs[-2], refs[-1]
    row = pl.program_id(0)
    groups, _, depth, inputs = xs.shape
    over = (((0,), (0,)), ((), ()))

    def block(d):
        return lax.rem(here_ref[0] - d + groups, groups) if slot else d

    @pl.when(live_ref[0] > slot)
    def _():
        @pl.when(row == 0)
        def _():
            each = direct_ref.shape[0] // groups
            for d in range(groups):
                mine = pl.ds(block(d) * each, each)
                xs[d, 0] = direct_ref[mine, 0].reshape(depth, inputs)
                if slot:
                    xs[d, 1] = others[d][...].reshape(depth, inputs)
                else:
                    xs[d, 1] = direct_ref[mine, 1].reshape(depth, inputs)

        r_a, m_a = xs[row, 0], xs[row, 1]
        left_re = jnp.concatenate([r_a, m_a], axis=0)
        left_im = jnp.concatenate([m_a, -r_a], axis=0)
        for d in range(groups):
            right = xs[d].reshape(2 * depth, inputs)
            cols = pl.ds(pl.multiple_of(block(d) * inputs, inputs), inputs)
            re = lax.dot_general(left_re, right, over, preferred_element_type=F32)
            im = lax.dot_general(left_im, right, over, preferred_element_type=F32)
            o_ref[0, 0, :, cols] = re * scale
            o_ref[0, 1, :, cols] = im * scale

    @pl.when(live_ref[0] <= slot)
    def _():
        o_ref[...] = jnp.zeros_like(o_ref)


def gram(here, live, direct, later, moved, groups, slot, slots, before):
    sources, _, frames, inputs = direct.shape
    chans = sources // groups
    total = groups * inputs
    depth = chans * frames
    back = lambda a, here: lax.rem(here[0] - a + groups, groups) if slot else a
    specs = [pl.BlockSpec((sources, 2 - slot, frames, inputs), lambda a, *_: (0, 2 * slot, 0, 0))]
    arrays = [direct]
    if slot:
        specs.append(pl.BlockSpec((chans, 1, frames, inputs), lambda a, *_: (0, 0, 0, 0)))
        arrays += [later, *moved]
        specs += [pl.BlockSpec(x.shape, lambda a, *_: (0, 0, 0)) for x in moved]
    more = [] if before is None else [before]
    return pl.pallas_call(
        functools.partial(gram_body, 1.0 / depth, slot),
        grid_spec=pltpu.PrefetchScalarGridSpec(
            num_scalar_prefetch=2,
            grid=(groups,),
            in_specs=specs + [pl.BlockSpec(memory_space=pl.ANY)] * len(more),
            out_specs=pl.BlockSpec(
                (1, 2, inputs, total), lambda a, here, live: (slot, 0, back(a, here), 0)
            ),
            scratch_shapes=[pltpu.VMEM((groups, 2, depth, inputs), BF16)],
        ),
        out_shape=jax.ShapeDtypeStruct((slots, 2, total, total), F32),
        input_output_aliases={2 + len(arrays): 0} if more else {},
        compiler_params=params(dimension_semantics=("arbitrary",)),
        cost_estimate=pl.CostEstimate(
            flops=8 * total * total * depth, bytes_accessed=12 * total * total, transcendentals=0
        ),
        name=f"gram_{slot}",
    )(here, live, *arrays, *more)


def shards(samples, gram_owner, beam_owner, delays, sections):
    input_count, frame_count, length_total = samples.shape
    half_count = length_total // 2
    inp_count = lax.axis_size("inp")
    chan_count = lax.axis_size("chan")
    inp_here = lax.axis_index("inp")
    chan_here = lax.axis_index("chan")
    owner_count = inp_count * chan_count
    gram_slots = 2 * gram_owner.shape[0] // owner_count
    beam_slots = 2 * half_count // chan_count
    section_width = delays.shape[0] // inp_count

    outgoing, later, spectra = channelize(
        samples, gram_owner, inp_here, owner_count, inp_count
    )
    arrived = lax.all_to_all(outgoing, ("inp", "chan"), split_axis=0, concat_axis=0, tiled=True)

    cosines, sines = phases(
        inp_here, sections, delays, input_count, section_width, 2.0 * math.pi / length_total
    )

    side = [(z, z ^ 1) for z in range(inp_count)]
    back = [(z, 3 - z) for z in range(inp_count)]
    parts = []
    near = []
    for first, count in CHANNEL_CHUNKS:
        keep, a, a2, b, b2 = beamform(spectra, cosines, sines, first, count)
        spectra, keep = lax.optimization_barrier((spectra, keep))
        parts.append((keep, a, a2, b, b2))
        if first + count < half_count:
            near.append((lax.ppermute(a, "inp", side), lax.ppermute(b, "inp", back)))
    later, arrived, parts, near = lax.optimization_barrier((later, arrived, parts, near))
    later = lax.all_to_all(later, "chan", split_axis=0, concat_axis=0, tiled=True)
    later = later.reshape(chan_count, inp_count, *later.shape[1:])
    near.append((lax.ppermute(parts[-1][1], "inp", side), lax.ppermute(parts[-1][3], "inp", back)))
    far = []
    for n, (_, _, a2, _, b2) in enumerate(parts):
        a_in, b_in = near[n]
        if far:
            a_in, b_in, far[-1] = lax.optimization_barrier((a_in, b_in, far[-1]))
        a_sum = (a2.astype(F32) + a_in[1].astype(F32)).astype(BF16)
        b_sum = (b2.astype(F32) + b_in[1].astype(F32)).astype(BF16)
        far.append((lax.ppermute(a_sum, "inp", back), lax.ppermute(b_sum, "inp", side)))
        near[n] = (a_in, b_in)
    leaving = None
    for (first, _), (keep, *_), (a_in, b_in), (a_far, b_far) in zip(CHANNEL_CHUNKS, parts, near, far):
        group = (keep, a_in, a_far, b_in, b_far)
        leaving = place(beam_owner, first, group, chan_count, beam_slots, leaving)
    leaving, later = lax.optimization_barrier((leaving, later))
    beams_in = lax.all_to_all(leaving, "chan", split_axis=0, concat_axis=0, tiled=True)

    here = inp_here * chan_count + chan_here
    gram_live = jnp.sum((gram_owner == here).astype(jnp.int32)).reshape(1)
    beam_live = jnp.sum((beam_owner == chan_here).astype(jnp.int32)).reshape(1)
    at = inp_here.reshape(1)
    moved = [
        lax.ppermute(later[:, d], "inp", [(z, (z + d) % inp_count) for z in range(inp_count)])
        for d in range(1, inp_count)
    ]
    visibilities = None
    for slot in range(gram_slots):
        visibilities = gram(
            at, gram_live, arrived, later, moved, inp_count, slot, gram_slots, visibilities
        )
    formed = deliver(beam_live, beams_in, chan_count, beam_slots)
    return (visibilities, formed[:, None])


def solution(mesh):
    return jax.shard_map(
        shards,
        mesh=mesh,
        in_specs=(P("inp", "chan", None), P(), P(), P(), P()),
        out_specs=(P(("inp", "chan"), None, None, None), P("chan", "inp", None, None)),
        check_vma=False,
    )
```

```python
import functools
import math

import jax
import jax.numpy as jnp
import ml_dtypes
import numpy as np
from jax import lax
from jax.experimental import pallas as pl
from jax.experimental.pallas import tpu as pltpu
from jax.sharding import PartitionSpec as P

BF16 = jnp.bfloat16
F32 = jnp.float32
VMEM_LIMIT = 56 * 1024 * 1024


def fourier_table(length_total):
    half_count = length_total // 2
    rows = np.arange(half_count, dtype=np.int32)
    cols = np.arange(length_total, dtype=np.int32)
    turns = (rows[:, None] * cols[None, :] % length_total).astype(np.float32)
    turns = turns * np.float32(2.0 * math.pi / length_total)
    factor = np.float32(1.0 / math.sqrt(length_total))
    both = np.stack([np.cos(turns) * factor, -np.sin(turns) * factor], axis=1)
    return both.reshape(length_total, length_total).astype(ml_dtypes.bfloat16)


def frame_major(frames):
    count = frames * frames
    matrix = np.zeros((count, count), np.float32)
    for f in range(frames):
        for i in range(frames):
            matrix[f * frames + i, i * frames + f] = 1.0
    return matrix.astype(ml_dtypes.bfloat16)


def params(**more):
    return pltpu.CompilerParams(vmem_limit_bytes=VMEM_LIMIT, **more)


def vmem():
    return pl.BlockSpec(memory_space=pltpu.VMEM)


def smem():
    return pl.BlockSpec(memory_space=pltpu.SMEM)


CHUNKS = 4
PIECE = 32


def channelize_body(
    groups, owner_ref, inp_ref, x_hbm, table_ref, perm_ref, gram_hbm, more_hbm, spec_hbm,
    x_ref, xs, rows, spec, taken, in_sem, gram_sem, spec_sem,
):
    frames, inputs, width = xs.shape
    channels = spec.shape[0]
    gram_channels = owner_ref.shape[0]
    group = frames * frames
    piece = inputs * frames // CHUNKS
    loads = []
    for c in range(CHUNKS):
        part = pl.ds(c * piece, piece)
        loads.append(pltpu.make_async_copy(x_hbm.at[part], x_ref.at[part], in_sem.at[c]))
        loads[-1].start()

    def clear(o, carry):
        taken[o] = 0
        return carry

    lax.fori_loop(0, taken.shape[0], clear, 0)

    def reorder(b, carry):
        block = x_ref[pl.ds(pl.multiple_of(b * group, group), group), :]
        moved = jnp.dot(perm_ref[...], block, preferred_element_type=F32)
        moved = moved.astype(BF16).reshape(frames, frames, width)
        xs[:, pl.ds(pl.multiple_of(b * frames, frames), frames), :] = moved
        return carry

    blocks = piece // group
    for c in range(CHUNKS):
        loads[c].wait()
        lax.fori_loop(c * blocks, (c + 1) * blocks, reorder, 0, unroll=True)

    def fetch(k):
        start = pl.multiple_of(k * 2 * frames, 2 * frames)
        both = [rows[h, pl.ds(start, 2 * frames), :] for h in range(inputs // 128)]
        return jnp.concatenate(both, axis=1).astype(BF16).reshape(2, frames, inputs)

    def low(k, carry):
        owner = owner_ref[k]
        slot = taken[owner]
        taken[owner] = slot + 1
        spec[k] = fetch(k)

        @pl.when(slot == 0)
        def _():
            both = gram_hbm.at[owner, pl.ds(0, 2)]
            pltpu.make_async_copy(spec.at[k], both, gram_sem).start()

        @pl.when(slot > 0)
        def _():
            chans = taken.shape[0] // groups
            ahead = lax.rem(lax.div(owner, chans) - inp_ref[0] + groups, groups)
            at = lax.rem(owner, chans) * groups + ahead
            pltpu.make_async_copy(spec.at[k, 0], gram_hbm.at[owner, 2], gram_sem).start()
            pltpu.make_async_copy(spec.at[k, 1], more_hbm.at[at], gram_sem).start()

        return carry

    def high(k, carry):
        spec[k] = fetch(k)
        return carry

    saves = []
    for start in range(0, channels, gram_channels):
        count = min(gram_channels, channels - start)

        def transform(f, carry, start=start, count=count):
            out = lax.dot_general(
                table_ref[2 * start : 2 * (start + count)],
                xs[f],
                (((1,), (1,)), ((), ())),
                preferred_element_type=F32,
            )
            for h in range(inputs // 128):
                at = pl.ds(f + 2 * start * frames, 2 * count, stride=frames)
                rows[h, at, :] = out[:, h * 128 : h * 128 + 128]
            return carry

        lax.fori_loop(0, frames, transform, 0, unroll=16)
        for k in range(start, start + count, PIECE):
            lax.fori_loop(k, k + PIECE, high if start else low, 0, unroll=4)
            part = pl.ds(k, PIECE)
            saves.append(pltpu.make_async_copy(spec.at[part], spec_hbm.at[part], spec_sem.at[k // PIECE]))
            saves[-1].start()
    all_low = pl.ds(0, gram_channels)
    pltpu.make_async_copy(spec.at[all_low], spec_hbm.at[all_low], gram_sem).wait()
    for save in saves:
        save.wait()


def channelize(samples, gram_owner, inp_here, owner_count, groups):
    inputs, frames, width = samples.shape
    channels = width // 2
    anywhere = pl.BlockSpec(memory_space=pl.ANY)
    return pl.pallas_call(
        functools.partial(channelize_body, groups),
        out_shape=(
            jax.ShapeDtypeStruct((owner_count, 3, frames, inputs), BF16),
            jax.ShapeDtypeStruct((owner_count, frames, inputs), BF16),
            jax.ShapeDtypeStruct((channels, 2, frames, inputs), BF16),
        ),
        in_specs=[smem(), smem(), anywhere, vmem(), vmem()],
        out_specs=(anywhere, anywhere, anywhere),
        scratch_shapes=[
            pltpu.VMEM((inputs * frames, width), BF16),
            pltpu.VMEM((frames, inputs, width), BF16),
            pltpu.VMEM((inputs // 128, 2 * channels * frames, 128), F32),
            pltpu.VMEM((channels, 2, frames, inputs), BF16),
            pltpu.SMEM((owner_count,), jnp.int32),
            pltpu.SemaphoreType.DMA((CHUNKS,)),
            pltpu.SemaphoreType.DMA(()),
            pltpu.SemaphoreType.DMA((channels // PIECE,)),
        ],
        compiler_params=params(),
        name="channelize",
    )(
        gram_owner,
        inp_here.reshape(1),
        samples.reshape(inputs * frames, width),
        jnp.asarray(fourier_table(width)),
        jnp.asarray(frame_major(frames)),
    )


def small_turn(angle):
    square = angle * angle
    cosine = sine = jnp.zeros_like(angle)
    for n in range(6, 0, -1):
        cosine = (cosine + (-1.0) ** n / math.factorial(2 * n)) * square
        sine = (sine + (-1.0) ** n / math.factorial(2 * n + 1)) * square
    return 1.0 + cosine, angle + angle * sine


def phase_body(
    factor, half, inp_ref, section_ref, delay_ref, cos_ref, sin_ref, turned
):
    here = inp_ref[0]
    near = jnp.bitwise_xor(here, 1)
    for q, device in enumerate((here, near, 3 - here, 3 - near)):

        def row(t, carry, q=q, device=device):
            beam = section_ref[device * half + t]
            turned[pl.ds(q * half + t, 1), :] = delay_ref[pl.ds(beam, 1), :]
            return carry

        lax.fori_loop(0, half, row, 0, unroll=8)
    for q in range(turned.shape[0] // half):
        cosines, sines = small_turn(turned[q * half : q * half + half] * factor)
        for source, target in ((cosines, cos_ref), (sines, sin_ref)):
            rows = jnp.concatenate([source, source], axis=0).T
            target[:, q * 2 * half : (q + 1) * 2 * half] = rows


def phases(inp_here, sections, delays, inputs, half, factor):
    beams = delays.shape[0]
    return pl.pallas_call(
        functools.partial(phase_body, factor, half),
        grid_spec=pltpu.PrefetchScalarGridSpec(
            num_scalar_prefetch=2,
            grid=(1,),
            in_specs=[pl.BlockSpec((beams, inputs), lambda g, inp, *_: (0, inp[0]))],
            out_specs=[
                pl.BlockSpec((inputs, 2 * beams), lambda g, *_: (0, 0)),
                pl.BlockSpec((inputs, 2 * beams), lambda g, *_: (0, 0)),
            ],
            scratch_shapes=[pltpu.VMEM((beams, inputs), F32)],
        ),
        out_shape=[jax.ShapeDtypeStruct((inputs, 2 * beams), F32)] * 2,
        compiler_params=params(),
        name="phases",
    )(inp_here.reshape(1), sections, delays)


STEP = 16
PAIR = 2 * STEP
CHANNEL_CHUNKS = ((0, 128), (128, 128))


def turn(a, b, c, s):
    return a * c - b * s, b * c + a * s


def beam_body(
    first, half, spec_ref, cos_ref, sin_ref, keep_ref, a_ref, a2_ref, b_ref, b2_ref,
    big_c, big_s, now_c, now_s, even, odd, stage,
):
    step = pl.program_id(0)
    last = pl.num_programs(0) - 1
    inputs, lanes = cos_ref.shape
    frames = keep_ref.shape[1]
    tiles = lanes // 128

    @pl.when(step == 0)
    def _():
        def start(r, carry):
            rows = pl.ds(pl.multiple_of(r * 16, 16), 16)
            for t in range(tiles):
                cols = pl.ds(t * 128, 128)
                c, s = cos_ref[rows, cols], sin_ref[rows, cols]
                done = 1
                while done < STEP // 2:
                    c, s = turn(c, s, c, s)
                    done *= 2
                mid = c, s
                c, s = turn(c, s, c, s)
                done *= 2
                big_c[rows, cols] = c
                big_s[rows, cols] = s
                while done <= first:
                    if first & done:
                        mid = turn(*mid, c, s)
                    c, s = turn(c, s, c, s)
                    done *= 2
                c, s = mid
                lane = lax.broadcasted_iota(jnp.int32, c.shape, 1)
                scale = 1.0 / 32.0
                now_c[rows, cols] = jnp.where(lane < half, c, -s) * scale
                now_s[rows, cols] = jnp.where(lane < half, s, c) * scale
            return carry

        lax.fori_loop(0, inputs // 16, start, 0)

    def make(r, weights):
        rows = pl.ds(pl.multiple_of(r * 16, 16), 16)
        a, b = now_c[rows], now_s[rows]
        c1, s1 = cos_ref[rows], sin_ref[rows]
        twice = c1 + c1
        p, q = a * c1, b * s1
        below, above = (a, p + q), (a, p - q)
        mid = STEP // 2
        weights[mid, rows] = a.astype(BF16)
        for m in range(1, mid + 1):
            weights[mid - m, rows] = below[1].astype(BF16)
            if m < mid:
                weights[mid + m, rows] = above[1].astype(BF16)
                below = below[1], twice * below[1] - below[0]
                above = above[1], twice * above[1] - above[0]
        now_c[rows], now_s[rows] = turn(a, b, big_c[rows], big_s[rows])

    lane = lax.broadcasted_iota(jnp.int32, (frames, 128), 1)
    sign = jnp.where(lane < half, -1.0, 1.0).astype(F32)

    def form(m, weights):
        got = jnp.dot(spec_ref[m], weights[m % STEP], preferred_element_type=F32)
        parts = []
        for t in range(tiles):
            real = got[:frames, t * 128 : t * 128 + 128]
            imag = got[frames:, t * 128 : t * 128 + 128]
            parts.append((real + sign * pltpu.roll(imag, half, 1)).astype(BF16))
        keep_ref[m] = parts[0]
        for t in range(1, tiles):
            stage[t - 1, m] = parts[t]

    @pl.when(step == 0)
    def _():
        @pl.loop(0, inputs // 16, unroll=2)
        def _(r):
            make(r, even)

    @pl.when(step > 0)
    def _():
        @pl.loop(0, STEP, unroll=True)
        def _(r):
            form(r, even)
            make(r, odd)

    @pl.when((step > 0) & (step < last))
    def _():
        @pl.loop(0, STEP, unroll=True)
        def _(r):
            form(STEP + r, odd)
            make(r, even)

    @pl.when(step == last)
    def _():
        @pl.loop(0, STEP, unroll=True)
        def _(r):
            form(STEP + r, odd)

    middle = last // 2

    @pl.when((step > 0) & (step <= middle))
    def _():
        a_ref[0], a_ref[1], a2_ref[...] = stage[0], stage[2], stage[1]

    @pl.when(step > middle)
    def _():
        b_ref[0], b_ref[1], b2_ref[...] = stage[1], stage[2], stage[0]


def beamform(spectra, cosines, sines, first, count):
    channels, _, frames, inputs = spectra.shape
    lanes = cosines.shape[1]
    part = count // 2
    tile = (frames, 128)
    steps = count // PAIR
    assert steps % 2 == 0 and inputs // 16 == STEP
    spectra = spectra.reshape(channels, 2 * frames, inputs)
    state = pltpu.VMEM((inputs, lanes), F32)
    at = lambda j: jnp.maximum(j - 1, 0)
    low = lambda j: jnp.minimum(at(j), steps // 2 - 1)
    high = lambda j: jnp.maximum(at(j) - steps // 2, 0)
    whole = lambda *shape: pl.BlockSpec(shape, lambda j: (0,) * len(shape))
    flops = count * 2 * (2 * frames) * inputs * lanes
    return pl.pallas_call(
        functools.partial(beam_body, first, 64),
        grid=(steps + 1,),
        out_shape=(
            jax.ShapeDtypeStruct((count, *tile), BF16),
            jax.ShapeDtypeStruct((2, part, *tile), BF16),
            jax.ShapeDtypeStruct((part, *tile), BF16),
            jax.ShapeDtypeStruct((2, part, *tile), BF16),
            jax.ShapeDtypeStruct((part, *tile), BF16),
        ),
        in_specs=[
            pl.BlockSpec((PAIR, 2 * frames, inputs), lambda j: (first // PAIR + at(j), 0, 0)),
            whole(inputs, lanes),
            whole(inputs, lanes),
        ],
        out_specs=(
            pl.BlockSpec((PAIR, *tile), lambda j: (at(j), 0, 0)),
            pl.BlockSpec((2, PAIR, *tile), lambda j: (0, low(j), 0, 0)),
            pl.BlockSpec((PAIR, *tile), lambda j: (low(j), 0, 0)),
            pl.BlockSpec((2, PAIR, *tile), lambda j: (0, high(j), 0, 0)),
            pl.BlockSpec((PAIR, *tile), lambda j: (high(j), 0, 0)),
        ),
        scratch_shapes=[
            state, state, state, state,
            pltpu.VMEM((STEP, inputs, lanes), BF16),
            pltpu.VMEM((STEP, inputs, lanes), BF16),
            pltpu.VMEM((lanes // 128 - 1, PAIR, *tile), BF16),
        ],
        compiler_params=params(dimension_semantics=("arbitrary",)),
        cost_estimate=pl.CostEstimate(
            flops=8 * flops, bytes_accessed=count * 2 * frames * inputs * 4, transcendentals=0
        ),
        name=f"beamform_{first}",
    )(spectra, cosines, sines)


def place_body(first, slots, owner_ref, keep, a_near, a_far, b_near, b_far, *rest):
    out_hbm, total, taken, sem = rest[-4:]
    part = a_far.shape[0]

    def clear(o, carry):
        taken[o] = 0
        return carry

    lax.fori_loop(0, taken.shape[0], clear, 0, unroll=8)

    def count(k, carry):
        taken[owner_ref[k]] = taken[owner_ref[k]] + 1
        return carry

    if first:
        lax.fori_loop(0, first, count, 0, unroll=8)
    for h, (near, far) in enumerate(((a_near, a_far), (b_near, b_far))):

        def body(n, carry, h=h, near=near, far=far):
            k = h * part + n
            owner = owner_ref[first + k]
            slot = taken[owner]
            taken[owner] = slot + 1
            value = keep[k].astype(F32) + near[0, n].astype(F32) + far[n].astype(F32)
            total[k] = value.astype(BF16)
            pltpu.make_async_copy(total.at[k], out_hbm.at[owner * slots + slot], sem).start()
            return carry

        lax.fori_loop(0, part, body, 0, unroll=8)
    pltpu.make_async_copy(total, out_hbm.at[pl.ds(0, 2 * part)], sem).wait()


def place(beam_owner, first, group, owner_count, slots, before):
    tile = group[0].shape[1:]
    count = group[0].shape[0]
    anywhere = pl.BlockSpec(memory_space=pl.ANY)

    def first_of(a):
        shape = (1, *a.shape[1:]) if a.ndim == 4 else a.shape
        return pl.BlockSpec(shape, lambda g: (0,) * len(shape))

    more = [] if before is None else [before]
    return pl.pallas_call(
        functools.partial(place_body, first, slots),
        grid=(1,),
        out_shape=jax.ShapeDtypeStruct((owner_count * slots, *tile), BF16),
        in_specs=[smem()] + [first_of(a) for a in group] + [anywhere] * len(more),
        out_specs=anywhere,
        scratch_shapes=[
            pltpu.VMEM((count, *tile), BF16),
            pltpu.SMEM((owner_count,), jnp.int32),
            pltpu.SemaphoreType.DMA(()),
        ],
        input_output_aliases={6: 0} if more else {},
        compiler_params=params(),
        name=f"place_beams_{first}",
    )(beam_owner, *group, *more)


def deliver_body(live_ref, x_any, o_ref, held, sem):
    _, sources, each, frames, lanes = held.shape
    step = pl.program_id(0)

    def fetch(n):
        at = lax.rem(n, 2)
        part = x_any.at[:, pl.ds(n * each, each)]
        return pltpu.make_async_copy(part, held.at[at], sem.at[at])

    @pl.when(step == 0)
    def _():
        fetch(step).start()

    @pl.when(step + 1 < pl.num_programs(0))
    def _():
        fetch(step + 1).start()

    fetch(step).wait()
    x_ref = held.at[lax.rem(step, 2)]
    for s in range(each):
        slot = pl.program_id(0) * each + s

        @pl.when(slot < live_ref[0])
        def _():
            o_ref[s] = x_ref[:, s].astype(F32).reshape(sources * frames, lanes)

        @pl.when(slot >= live_ref[0])
        def _():
            o_ref[s] = jnp.zeros((sources * frames, lanes), F32)


def deliver(live, arrived, sources, slots):
    _, frames, lanes = arrived.shape
    each = 4
    return pl.pallas_call(
        deliver_body,
        grid=(slots // each,),
        out_shape=jax.ShapeDtypeStruct((slots, sources * frames, lanes), F32),
        in_specs=[
            smem(),
            pl.BlockSpec(memory_space=pl.ANY),
        ],
        out_specs=pl.BlockSpec((each, sources * frames, lanes), lambda s: (s, 0, 0)),
        scratch_shapes=[
            pltpu.VMEM((2, sources, each, frames, lanes), BF16),
            pltpu.SemaphoreType.DMA((2,)),
        ],
        compiler_params=pltpu.CompilerParams(
            vmem_limit_bytes=VMEM_LIMIT // 4, dimension_semantics=("arbitrary",)
        ),
        name="deliver_beams",
    )(live, arrived.reshape(sources, slots, frames, lanes))


def gram_body(scale, slot, here_ref, live_ref, direct_ref, *refs):
    others, o_ref, xs = refs[:4], refs[-2], refs[-1]
    row = pl.program_id(0)
    groups, _, depth, inputs = xs.shape
    over = (((0,), (0,)), ((), ()))

    def block(d):
        return lax.rem(here_ref[0] - d + groups, groups) if slot else d

    @pl.when(live_ref[0] > slot)
    def _():
        @pl.when(row == 0)
        def _():
            each = direct_ref.shape[0] // groups
            for d in range(groups):
                mine = pl.ds(block(d) * each, each)
                xs[d, 0] = direct_ref[mine, 0].reshape(depth, inputs)
                if slot:
                    xs[d, 1] = others[d][...].reshape(depth, inputs)
                else:
                    xs[d, 1] = direct_ref[mine, 1].reshape(depth, inputs)

        r_a, m_a = xs[row, 0], xs[row, 1]
        left_re = jnp.concatenate([r_a, m_a], axis=0)
        left_im = jnp.concatenate([m_a, -r_a], axis=0)
        for d in range(groups):
            right = xs[d].reshape(2 * depth, inputs)
            cols = pl.ds(pl.multiple_of(block(d) * inputs, inputs), inputs)
            re = lax.dot_general(left_re, right, over, preferred_element_type=F32)
            im = lax.dot_general(left_im, right, over, preferred_element_type=F32)
            o_ref[0, 0, :, cols] = re * scale
            o_ref[0, 1, :, cols] = im * scale

    @pl.when(live_ref[0] <= slot)
    def _():
        o_ref[...] = jnp.zeros_like(o_ref)


def gram(here, live, direct, later, moved, groups, slot, slots, before):
    sources, _, frames, inputs = direct.shape
    chans = sources // groups
    total = groups * inputs
    depth = chans * frames
    back = lambda a, here: lax.rem(here[0] - a + groups, groups) if slot else a
    specs = [pl.BlockSpec((sources, 2 - slot, frames, inputs), lambda a, *_: (0, 2 * slot, 0, 0))]
    arrays = [direct]
    if slot:
        specs.append(pl.BlockSpec((chans, 1, frames, inputs), lambda a, *_: (0, 0, 0, 0)))
        arrays += [later, *moved]
        specs += [pl.BlockSpec(x.shape, lambda a, *_: (0, 0, 0)) for x in moved]
    more = [] if before is None else [before]
    return pl.pallas_call(
        functools.partial(gram_body, 1.0 / depth, slot),
        grid_spec=pltpu.PrefetchScalarGridSpec(
            num_scalar_prefetch=2,
            grid=(groups,),
            in_specs=specs + [pl.BlockSpec(memory_space=pl.ANY)] * len(more),
            out_specs=pl.BlockSpec(
                (1, 2, inputs, total), lambda a, here, live: (slot, 0, back(a, here), 0)
            ),
            scratch_shapes=[pltpu.VMEM((groups, 2, depth, inputs), BF16)],
        ),
        out_shape=jax.ShapeDtypeStruct((slots, 2, total, total), F32),
        input_output_aliases={2 + len(arrays): 0} if more else {},
        compiler_params=params(dimension_semantics=("arbitrary",)),
        cost_estimate=pl.CostEstimate(
            flops=8 * total * total * depth, bytes_accessed=12 * total * total, transcendentals=0
        ),
        name=f"gram_{slot}",
    )(here, live, *arrays, *more)


def shards(samples, gram_owner, beam_owner, delays, sections):
    input_count, frame_count, length_total = samples.shape
    half_count = length_total // 2
    inp_count = lax.axis_size("inp")
    chan_count = lax.axis_size("chan")
    inp_here = lax.axis_index("inp")
    chan_here = lax.axis_index("chan")
    owner_count = inp_count * chan_count
    gram_slots = 2 * gram_owner.shape[0] // owner_count
    beam_slots = 2 * half_count // chan_count
    section_width = delays.shape[0] // inp_count

    outgoing, later, spectra = channelize(
        samples, gram_owner, inp_here, owner_count, inp_count
    )
    arrived = lax.all_to_all(outgoing, ("inp", "chan"), split_axis=0, concat_axis=0, tiled=True)

    cosines, sines = phases(
        inp_here, sections, delays, input_count, section_width, 2.0 * math.pi / length_total
    )

    side = [(z, z ^ 1) for z in range(inp_count)]
    back = [(z, 3 - z) for z in range(inp_count)]
    parts = []
    near = []
    for first, count in CHANNEL_CHUNKS:
        keep, a, a2, b, b2 = beamform(spectra, cosines, sines, first, count)
        spectra, keep = lax.optimization_barrier((spectra, keep))
        parts.append((keep, a, a2, b, b2))
        if first + count < half_count:
            near.append((lax.ppermute(a, "inp", side), lax.ppermute(b, "inp", back)))
    last = parts[-1]
    later, arrived, parts, near = lax.optimization_barrier((later, arrived, parts, near))
    later = lax.all_to_all(later, "chan", split_axis=0, concat_axis=0, tiled=True)
    later = later.reshape(chan_count, inp_count, *later.shape[1:])
    near.append((lax.ppermute(last[1], "inp", side), lax.ppermute(last[3], "inp", back)))
    far = []
    for n, (_, _, a2, _, b2) in enumerate(parts):
        a_in, b_in = near[n]
        if far:
            a_in, b_in, far[-1] = lax.optimization_barrier((a_in, b_in, far[-1]))
        a_sum = (a2.astype(F32) + a_in[1].astype(F32)).astype(BF16)
        b_sum = (b2.astype(F32) + b_in[1].astype(F32)).astype(BF16)
        far.append((lax.ppermute(a_sum, "inp", back), lax.ppermute(b_sum, "inp", side)))
        near[n] = (a_in, b_in)
    leaving = None
    for (first, _), (keep, *_), (a_in, b_in), (a_far, b_far) in zip(CHANNEL_CHUNKS, parts, near, far):
        group = (keep, a_in, a_far, b_in, b_far)
        leaving = place(beam_owner, first, group, chan_count, beam_slots, leaving)
    leaving, later = lax.optimization_barrier((leaving, later))
    beams_in = lax.all_to_all(leaving, "chan", split_axis=0, concat_axis=0, tiled=True)

    here = inp_here * chan_count + chan_here
    gram_live = jnp.sum((gram_owner == here).astype(jnp.int32)).reshape(1)
    beam_live = jnp.sum((beam_owner == chan_here).astype(jnp.int32)).reshape(1)
    at = inp_here.reshape(1)
    moved = [
        lax.ppermute(later[:, d], "inp", [(z, (z + d) % inp_count) for z in range(inp_count)])
        for d in range(1, inp_count)
    ]
    visibilities = None
    for slot in range(gram_slots):
        visibilities = gram(
            at, gram_live, arrived, later, moved, inp_count, slot, gram_slots, visibilities
        )
    formed = deliver(beam_live, beams_in, chan_count, beam_slots)
    return (visibilities, formed[:, None])


def solution(mesh):
    return jax.shard_map(
        shards,
        mesh=mesh,
        in_specs=(P("inp", "chan", None), P(), P(), P(), P()),
        out_specs=(P(("inp", "chan"), None, None, None), P("chan", "inp", None, None)),
        check_vma=False,
    )
```
